256 devices in a mesh: dp: 4 (over y), expert: 16 (over z, core), ffn: 4 (over x).
Axes of the slice: x: 4, y: 4, z: 8, core: 2. Of those that a mesh axis runs over, the one named last changes fastest.
Arguments:
- tokens: bfloat16 [8192, 7168], P(('dp', 'expert'), 'ffn'), may hold values from -6 to 6
- grad_out: bfloat16 [8192, 7168], P(('dp', 'expert'), 'ffn'), may hold values from -3 to 3
- route_ids: int32 [8192, 2], P(('dp', 'expert')), may hold values from 0 to 15, all different within a row; in each aligned block of 128 rows (0 to 127, 128 to 255, ...) at most 20 rows name the same one
- combine: float32 [8192, 2], P(('dp', 'expert')), may hold values from 0.2 to 1
- gate_weight: bfloat16 [16, 7168, 1024], P('expert', 'dp', 'ffn'), may hold values from -0.0625 to 0.0625
- up_weight: bfloat16 [16, 7168, 1024], P('expert', 'dp', 'ffn'), may hold values from -0.0625 to 0.0625
- down_weight: bfloat16 [16, 1024, 7168], P('expert', 'ffn', 'dp'), may hold values from -0.1875 to 0.1875
Outputs:
- grad_tokens: bfloat16 [8192, 7168], P(('dp', 'expert'), 'ffn')
- grad_gate: float32 [16, 7168, 1024], P('expert', 'dp', 'ffn')
- grad_up: float32 [16, 7168, 1024], P('expert', 'dp', 'ffn')
- grad_down: float32 [16, 1024, 7168], P('expert', 'ffn', 'dp')
The draws below stay inside these ranges and needn't reach their ends.
Inputs may be any that keep to these rules, and one draw needn't show every extreme that they name: `route_ids`: each row names 2 different experts; every expert is named by some row. In each aligned block of 128 rows (the rows of one device) no expert is named by more than 20 rows, a bound that some block reaches.
All inputs are finite; a program needn't handle non-finite values.
Results may differ from the reference program's by a relative error of at most 0.019.
Values may be sent and summed in bfloat16 or wider, within the bound.
No kernel may reach another device: no remote copies, remote signals or barrier semaphores. Data moves between devices by JAX's collectives and lax.ppermute only.
A program may use at most 128 MiB of HBM per device.

```python
import math
import jax
import jax.numpy as jnp
import numpy as np
from jax import lax

D = 7168
FF = 1024
TOP = 2
TOK_DEV = 128
EXPERTS = 16
TOKENS = 8192
CAP = 20
N_DP = 4
N_EXPERT = 16
N_FFN = 4


def block_levels(key, extent, split, smallest, largest):
    level, own = 1.0, jax.random.fold_in(key, 6)
    for axis_at, blocks in split:
        heights = jnp.exp(jax.random.uniform(jax.random.fold_in(own, axis_at), (blocks,), jnp.float32, smallest / len(split), largest / len(split)))
        level = level * jnp.repeat(heights, extent[axis_at] // blocks).reshape([-1 if axis == axis_at else 1 for axis in range(len(extent))])
    return level


def deal_out(stream_key, own, number, rows, count, top, reach, slope):
    sequence = jax.random.permutation(stream_key, count)
    crowded, common = portions_of(count, rows * top, reach, slope, True), portions_of(count, rows * top, reach, slope, False)
    places = jnp.arange(count)

    def named(tallies, turn):
        used = int((tallies > 0).sum())
        fixed = max(1, used // 4)
        moved = fixed + (places - fixed + turn * (used - fixed)) % max(1, count - fixed)
        return jnp.zeros((count,), jnp.int32).at[sequence[jnp.where(places < fixed, places, moved)]].set(jnp.asarray(tallies, jnp.int32))

    tallies = jnp.where(number % 4 == 0, named(crowded, number // 4), named(common, number - number // 4 - 1))
    mixed = jax.random.permutation(jax.random.fold_in(own, 3), count)
    giver, receiver = mixed[0:count // 2 * 2:2], mixed[1:count // 2 * 2:2]
    margin = jnp.minimum(tallies[giver] - 1, reach - tallies[receiver]) // 2
    margin = jnp.where((giver == sequence[0]) | (receiver == sequence[0]) | (tallies[receiver] == 0), 0, jnp.maximum(margin, 0))
    moved = jax.random.randint(jax.random.fold_in(own, 4), (count // 2,), 0, 1 << 20) % (margin + 1)
    tallies = tallies.at[giver].add(-moved).at[receiver].add(moved)
    members = jnp.searchsorted(jnp.cumsum(tallies), jnp.arange(rows * top), side="right").astype(jnp.int32)
    listing = members.reshape(top, rows).T
    listing = listing[jax.random.permutation(jax.random.fold_in(own, 1), rows)]
    turn = jax.random.randint(jax.random.fold_in(own, 2), (rows, 1), 0, top)
    return jnp.take_along_axis(listing, (jnp.arange(top)[None, :] + turn) % top, axis=1)


def portions_of(number_of, total, most, lean, full):
    portions = [(1 << 20) // math.isqrt(grade ** lean) + 1 for grade in range(1, number_of + 1)]
    largest = most if full else min(most, max(-(-total // number_of), total * portions[0] // sum(portions)))
    least = 1 if total - largest >= number_of - 1 else 0
    counts, rest = [largest] + [least] * (number_of - 1), total - largest - least * (number_of - 1)
    while rest > 0:
        free = [i for i in range(1, number_of) if counts[i] < largest] or [i for i in range(1, number_of) if counts[i] < most]
        pool, budget = sum([portions[i] for i in free]), rest
        for i in free:
            addition = min(most - counts[i], max(1, budget * portions[i] // pool), rest)
            counts[i] = counts[i] + addition
            rest = rest - addition
    return np.array(counts)


def gaussian(own_key, extent, spread, bound, cuts=(), held_as=jnp.bfloat16):
    drawn = jax.random.normal(own_key, extent, jnp.float32) * spread
    if len(cuts) > 0:
        drawn = block_levels(own_key, extent, cuts, -0.22, 0.18) * drawn
    return jnp.clip(drawn, min=-bound, max=bound).astype(held_as)


def setup_inputs(seed: int = 0) -> dict:
    key_of = jax.random.split(jax.random.key(seed), 8)
    tokens = gaussian(key_of[0], (TOKENS, D), 1.0, 6.0, ((0, 64), (1, 4)))
    grad_out = gaussian(key_of[1], (TOKENS, D), 0.5, 3.0, ((0, 64), (1, 4)))
    route_ids_keys = jax.random.split(jax.random.fold_in(key_of[2], 1), TOKENS // TOK_DEV)
    route_ids_turns = jax.random.permutation(jax.random.fold_in(key_of[2], 3), TOKENS // TOK_DEV)
    route_ids = jax.vmap(lambda own, number: deal_out(jax.random.fold_in(key_of[2], 2), own, number, TOK_DEV, EXPERTS, TOP, CAP, 2))(route_ids_keys, route_ids_turns).reshape((TOKENS, TOP))
    combine = jnp.clip(0.2 + 0.8 * jax.random.uniform(key_of[3], (TOKENS, TOP), jnp.float32) ** block_levels(key_of[3], (TOKENS, TOP), ((0, 64),), -0.2, 0.2), 0.2, 1.0)
    gate_weight = gaussian(key_of[4], (EXPERTS, D, FF), D ** -0.5, 0.0625, ((0, 16), (1, 4), (2, 4)))
    up_weight = gaussian(key_of[5], (EXPERTS, D, FF), D ** -0.5, 0.0625, ((0, 16), (1, 4), (2, 4)))
    down_weight = gaussian(key_of[6], (EXPERTS, FF, D), FF ** -0.5, 0.1875, ((0, 16), (1, 4), (2, 4)))
    return dict(tokens=tokens, grad_out=grad_out, route_ids=route_ids, combine=combine, gate_weight=gate_weight, up_weight=up_weight, down_weight=down_weight)


def reference(tokens, grad_out, route_ids, combine, gate_weight, up_weight, down_weight):
    slots_all = TOKENS * TOP
    blocks = N_DP * N_EXPERT
    per_block = TOK_DEV * TOP
    rows_exp = N_EXPERT * CAP
    groups_width = FF // N_FFN
    expert_of = route_ids.reshape(slots_all).astype(jnp.int32)
    onehot = (expert_of[:, None] == jnp.arange(EXPERTS, dtype=jnp.int32)[None, :]).astype(jnp.int32)
    onehot = onehot.reshape(blocks, per_block, EXPERTS)
    earlier = jnp.cumsum(onehot, axis=1) - onehot
    position = jnp.sum(earlier * onehot, axis=2).reshape(slots_all).astype(jnp.int32)
    block_of = (jnp.arange(slots_all, dtype=jnp.int32) // per_block).astype(jnp.int32)
    dest = ((expert_of * blocks + block_of) * CAP + position).astype(jnp.int32)
    table = jnp.full((EXPERTS * blocks * CAP,), slots_all, jnp.int32)
    table = table.at[dest].set(jnp.arange(slots_all, dtype=jnp.int32))
    table = table.reshape(EXPERTS, N_DP, rows_exp)
    padded_tok = jnp.concatenate([tokens, jnp.zeros((1, D), tokens.dtype)], axis=0)
    scaled = (combine[:, :, None] * grad_out[:, None, :].astype(jnp.float32)).astype(jnp.bfloat16)
    padded_z = jnp.concatenate([scaled.reshape(slots_all, D), jnp.zeros((1, D), jnp.bfloat16)], axis=0)

    def one_expert(items):
        index, w_gate, w_up, w_down = items
        x_rows = padded_tok[(index // TOP).astype(jnp.int32)].reshape(N_DP * rows_exp, D)
        z_rows = padded_z[index].reshape(N_DP * rows_exp, D)
        gate = jnp.dot(x_rows, w_gate, preferred_element_type=jnp.float32)
        up = jnp.dot(x_rows, w_up, preferred_element_type=jnp.float32)
        sig = jax.nn.sigmoid(gate)
        hidden = (gate * sig * up).astype(jnp.bfloat16)
        grad_hidden = jnp.dot(z_rows, w_down.T, preferred_element_type=jnp.float32)
        grad_up_act = (grad_hidden * gate * sig).astype(jnp.bfloat16)
        grad_gate_act = (grad_hidden * up * sig * (1.0 + gate * (1.0 - sig))).astype(jnp.bfloat16)
        x3 = x_rows.reshape(N_DP, rows_exp, D).astype(jnp.float32)
        z3 = z_rows.reshape(N_DP, rows_exp, D).astype(jnp.float32)
        gg = jnp.einsum('nrd,nrf->ndf', x3, grad_gate_act.reshape(N_DP, rows_exp, FF).astype(jnp.float32))
        gu = jnp.einsum('nrd,nrf->ndf', x3, grad_up_act.reshape(N_DP, rows_exp, FF).astype(jnp.float32))
        gd = jnp.einsum('nrf,nrd->nfd', hidden.reshape(N_DP, rows_exp, FF).astype(jnp.float32), z3)
        gg = jnp.sum(gg.astype(jnp.bfloat16).astype(jnp.float32), axis=0)
        gu = jnp.sum(gu.astype(jnp.bfloat16).astype(jnp.float32), axis=0)
        gd = jnp.sum(gd.astype(jnp.bfloat16).astype(jnp.float32), axis=0)
        rows_all = N_DP * rows_exp
        dg3 = grad_gate_act.reshape(rows_all, N_FFN, groups_width).astype(jnp.float32)
        du3 = grad_up_act.reshape(rows_all, N_FFN, groups_width).astype(jnp.float32)
        wg3 = w_gate.reshape(D, N_FFN, groups_width).astype(jnp.float32)
        wu3 = w_up.reshape(D, N_FFN, groups_width).astype(jnp.float32)
        partial_sum = jnp.einsum('mnf,dnf->nmd', dg3, wg3) + jnp.einsum('mnf,dnf->nmd', du3, wu3)
        rounded = lax.optimization_barrier(partial_sum.astype(jnp.bfloat16))
        slot_grad = jnp.sum(rounded.astype(jnp.float32), axis=0).astype(jnp.bfloat16)
        return slot_grad, gg, gu, gd

    slot_grads, grad_gate, grad_up, grad_down = lax.map(one_expert, (table, gate_weight, up_weight, down_weight))
    gathered = jnp.zeros((slots_all + 1, D), jnp.float32)
    gathered = gathered.at[table.reshape(-1)].add(slot_grads.reshape(-1, D).astype(jnp.float32))
    grad_tokens = jnp.sum(gathered[:slots_all].reshape(TOKENS, TOP, D), axis=1).astype(jnp.bfloat16)
    return grad_tokens, grad_gate, grad_up, grad_down
```

```python
import jax
import jax.numpy as jnp
from jax import lax
from jax.sharding import PartitionSpec as P

F32 = jnp.float32
BF16 = jnp.bfloat16


def dot(a, b, contract):
    return lax.dot_general(a, b, (contract, ((), ())), preferred_element_type=F32)


def activations(gate, up, grad_hidden):
    sig = jax.nn.sigmoid(gate)
    hidden = (gate * sig * up).astype(BF16)
    grad_up_act = (grad_hidden * gate * sig).astype(BF16)
    grad_gate_act = (grad_hidden * up * sig * (1.0 + gate * (1.0 - sig))).astype(BF16)
    return hidden, grad_up_act, grad_gate_act


def slots_of(route, experts, capacity):
    rows, top = route.shape
    expert_of = route.reshape(rows * top)
    onehot = (expert_of[:, None] == jnp.arange(experts, dtype=jnp.int32)[None, :]).astype(jnp.int32)
    earlier = jnp.cumsum(onehot, axis=0) - onehot
    position = jnp.sum(earlier * onehot, axis=1)
    return (expert_of * capacity + position).reshape(rows, top)


def per_device(tokens, grad_out, route_ids, combine, gate_weight, up_weight, down_weight):
    rows, width = tokens.shape
    top = route_ids.shape[1]
    groups = lax.axis_size("expert")
    n = lax.axis_size("ffn")
    experts = gate_weight.shape[0] * groups
    capacity = min(rows, (5 * top * rows + 4 * experts - 1) // (4 * experts))
    slots = experts * capacity
    half = width // 2
    units = gate_weight.shape[2]
    me = lax.axis_index("ffn")
    mid = slots // 2

    def shift(x, by):
        return lax.ppermute(x, "ffn", [(i, (i + by) % n) for i in range(n)])

    def flip(x):
        return lax.ppermute(
            x, ("dp", "ffn"), [(a * n + b, b * n + a) for a in range(n) for b in range(n)]
        )

    def exchange(x):
        out = lax.all_to_all(
            x.reshape(groups, capacity, x.shape[1]), "expert", split_axis=0, concat_axis=0, tiled=True
        )
        return out.reshape(slots, x.shape[1])

    def gather_rows(x):
        left, right = shift(x, 1), shift(x, -1)
        far = jnp.concatenate([shift(left[:mid], 1), shift(right[mid:], -1)], axis=0)
        out = jnp.zeros((n,) + x.shape, x.dtype)
        for by, part in ((0, x), (n - 1, left), (1, right), (2, far)):
            out = lax.dynamic_update_slice(out, part[None], ((me + by) % n, 0, 0))
        return out

    w_in = jnp.concatenate([gate_weight[0], up_weight[0]], axis=1)
    w_in = lax.all_gather(w_in, "dp", axis=0, tiled=False)

    z_local = flip(grad_out)
    routing = jnp.concatenate([route_ids.astype(F32), combine], axis=1)
    routing = flip(routing)
    z_slot = slots_of(routing[:, :top].astype(jnp.int32), experts, capacity)
    x_slot = slots_of(route_ids, experts, capacity)

    slot_index = jnp.arange(slots, dtype=jnp.int32)[:, None]

    def placed(slot, k):
        return slot_index == slot[:, k][None, :]

    x_place = sum(placed(x_slot, k).astype(BF16) for k in range(top))
    z_place = sum(placed(z_slot, k).astype(BF16) for k in range(top))
    z_scale = sum(
        jnp.sum(jnp.where(placed(z_slot, k), routing[:, top + k][None, :], 0.0), axis=1) for k in range(top)
    )[:, None]

    def pack_x(h):
        return dot(x_place, tokens[:, h * half : (h + 1) * half], ((1,), (0,))).astype(BF16)

    def pack_z(h):
        return (dot(z_place, z_local[:, h * half : (h + 1) * half], ((1,), (0,))) * z_scale).astype(BF16)

    x_0 = gather_rows(exchange(pack_x(0)))
    z_0 = gather_rows(exchange(pack_z(0)))
    z_1 = gather_rows(exchange(pack_z(1)))
    x_1 = gather_rows(exchange(pack_x(1)))
    xs, zs = (x_0, x_1), (z_0.reshape(n * slots, half), z_1.reshape(n * slots, half))

    w_down = down_weight[0]
    grad_hidden = sum(dot(zs[h], w_down[:, h * half : (h + 1) * half], ((1,), (1,))) for h in range(2))
    grad_hidden = lax.psum_scatter(grad_hidden.astype(BF16), "dp", scatter_dimension=0, tiled=True)

    both = sum(
        dot(xs[h][q], w_in[q, h * half : (h + 1) * half], ((1,), (0,))) for h in range(2) for q in range(n)
    )
    hidden, grad_up_act, grad_gate_act = activations(both[:, :units], both[:, units:], grad_hidden.astype(F32))
    hidden_all = lax.all_gather(hidden, "dp", axis=0, tiled=True)
    acts = jnp.concatenate([grad_gate_act, grad_up_act], axis=1)

    def weight_grad(act):
        part = jnp.stack(
            [
                jnp.concatenate([dot(xs[h][q], act, ((0,), (0,))).astype(BF16) for h in range(2)], axis=0)
                for q in range(n)
            ]
        )
        return lax.psum_scatter(part, "dp", scatter_dimension=0, tiled=True).astype(F32)

    def input_grad(h):
        def partial(by):
            w = lax.dynamic_slice(w_in, ((me + by) % n, h * half, 0), (1, half, 2 * units))[0]
            return dot(acts, w, ((1,), (1,)))

        far = partial(2).astype(BF16)
        from_left, from_right = shift(far[:mid], 1), shift(far[mid:], -1)
        right, left = partial(1), partial(n - 1)
        right = jnp.concatenate([right[:mid] + from_left.astype(F32), right[mid:]], axis=0).astype(BF16)
        left = jnp.concatenate([left[:mid], left[mid:] + from_right.astype(F32)], axis=0).astype(BF16)
        total = partial(0) + shift(right, 1).astype(F32) + shift(left, -1).astype(F32)
        back = exchange(total.astype(BF16))
        return dot(x_place, back, ((0,), (0,))).astype(BF16)

    grad_gate = weight_grad(grad_gate_act)
    grad_tokens = jnp.concatenate([input_grad(0), input_grad(1)], axis=1)
    grad_up = weight_grad(grad_up_act)
    grad_down = jnp.concatenate([dot(hidden_all, zs[h], ((0,), (0,))) for h in range(2)], axis=1)[None]
    return grad_tokens, grad_gate, grad_up, grad_down


def solution(mesh):
    return jax.shard_map(
        per_device,
        mesh=mesh,
        in_specs=(
            P(("dp", "expert"), "ffn"),
            P(("dp", "expert"), "ffn"),
            P(("dp", "expert"), None),
            P(("dp", "expert"), None),
            P("expert", "dp", "ffn"),
            P("expert", "dp", "ffn"),
            P("expert", "ffn", "dp"),
        ),
        out_specs=(
            P(("dp", "expert"), "ffn"),
            P("expert", "dp", "ffn"),
            P("expert", "dp", "ffn"),
            P("expert", "ffn", "dp"),
        ),
        check_vma=False,
    )
```

```python
import jax
import jax.numpy as jnp
from jax import lax
from jax.experimental import pallas as pl
from jax.experimental.pallas import tpu as pltpu
from jax.sharding import PartitionSpec as P

F32 = jnp.float32
BF16 = jnp.bfloat16
N = 4
ANY = pl.BlockSpec(memory_space=pl.ANY)
SMEM = pl.BlockSpec(memory_space=pltpu.SMEM)


def dot(a, b, contract):
    return lax.dot_general(a, b, (contract, ((), ())), preferred_element_type=F32)


NN, NT, TN = ((1,), (0,)), ((1,), (1,)), ((0,), (0,))


def call(body, outs, scratch, args, copies, smem=0):
    return pl.pallas_call(
        body,
        out_shape=outs,
        in_specs=[SMEM] * smem + [ANY] * (len(args) - smem),
        out_specs=jax.tree.map(lambda _: ANY, outs),
        scratch_shapes=list(scratch) + [pltpu.SemaphoreType.DMA((copies,))],
    )(*args)


class Copies:
    def __init__(self, sems):
        self.sems, self.used = sems, 0

    def start(self, src, dst):
        copy = pltpu.make_async_copy(src, dst, self.sems.at[self.used])
        self.used += 1
        copy.start()
        return copy


def other(at_ref, by):
    return (at_ref[0] + by) & (N - 1)


def project(parts, w_in, at, offset, base=None, grads=None):
    rows, width = parts[0][0].shape
    cols = w_in.shape[2]
    units = cols // 2

    def body(at_ref, w_ref, *refs):
        x_refs, refs = refs[: 2 * N], refs[2 * N :]
        extra, refs = refs[: 0 if base is None else 1 + N], refs[0 if base is None else 1 + N :]
        outs = refs[:1] if base is None else refs[:2]
        refs = refs[len(outs) :]
        w_buf, x_buf, out_bufs, sems = refs[0], refs[1], refs[2 : 2 + len(outs)], refs[-1]
        copies = Copies(sems)
        loads = []
        for j in range(N):
            loads.append(
                [copies.start(w_ref.at[other(at_ref, j), pl.ds(offset, 2 * width)], w_buf.at[j])]
                + [copies.start(x_refs[2 * j + c], x_buf.at[2 * j + c]) for c in range(2)]
            )
        if base is not None:
            base_buf, grad_buf = refs[4], refs[5]
            more = [copies.start(extra[0], base_buf)]
            more += [copies.start(extra[1 + j], grad_buf.at[j]) for j in range(N)]
        total = None
        for j in range(N):
            for copy in loads[j]:
                copy.wait()
            for c in range(2):
                term = dot(x_buf[2 * j + c], w_buf[j, c * width : (c + 1) * width], NN)
                total = term if total is None else total + term
        if base is None:
            out_bufs[0][...] = total
        else:
            for copy in more:
                copy.wait()
            total = total + base_buf[...]
            grad = sum(grad_buf[j].astype(F32) for j in range(N))
            gate, up = total[:, :units], total[:, units:]
            sig = jax.nn.sigmoid(gate)
            out_bufs[0][...] = (gate * sig * up).astype(BF16)
            out_bufs[1][:, :units] = (grad * up * sig * (1.0 + gate * (1.0 - sig))).astype(BF16)
            out_bufs[1][:, units:] = (grad * gate * sig).astype(BF16)
        stores = [copies.start(b, o) for b, o in zip(out_bufs, outs)]
        for copy in stores:
            copy.wait()

    flat = [x for pair in parts for x in pair]
    scratch = [pltpu.VMEM((N, 2 * width, cols), BF16), pltpu.VMEM((2 * N, rows, width), BF16)]
    if base is None:
        outs = (jax.ShapeDtypeStruct((rows, cols), F32),)
        scratch += [pltpu.VMEM((rows, cols), F32)]
        return call(body, outs, scratch, [at, w_in] + flat, 3 * N + 1, 1)[0]
    outs = (jax.ShapeDtypeStruct((rows, units), BF16), jax.ShapeDtypeStruct((rows, cols), BF16))
    scratch += [pltpu.VMEM((rows, units), BF16), pltpu.VMEM((rows, cols), BF16)]
    scratch += [pltpu.VMEM((rows, cols), F32), pltpu.VMEM((N, rows, units), BF16)]
    return call(body, outs, scratch, [at, w_in] + flat + [base] + grads, 3 * N + 1 + N + 2, 1)


def hidden_grads(chunks, w_down, at):
    rows = chunks[0][0][0].shape[0]
    units, width = w_down.shape
    flat = [x for parts in chunks for pair in parts for x in pair]

    def body(at_ref, w_ref, *refs):
        x_refs, out, refs = refs[: len(flat)], refs[len(flat)], refs[len(flat) + 1 :]
        w_buf, x_bufs, out_buf, sems = refs[0], refs[1:-2], refs[-2], refs[-1]
        copies = Copies(sems)
        first = copies.start(w_ref, w_buf)
        loads = [copies.start(src, dst) for src, dst in zip(x_refs, x_bufs)]
        first.wait()
        stores = []
        for j in range(N):
            total, lo = None, 0
            for h in range(len(chunks)):
                for c in range(2):
                    i = (h * N + j) * 2 + c
                    w = x_bufs[i].shape[1]
                    loads[i].wait()
                    term = dot(x_bufs[i][...], w_buf[:, lo : lo + w], NT)
                    total = term if total is None else total + term
                    lo += w
            out_buf[j] = total.astype(BF16)
            stores.append(copies.start(out_buf.at[j], out.at[(at_ref[0] + j - at_ref[1]) & (N - 1)]))
        for copy in stores:
            copy.wait()

    return call(
        body,
        jax.ShapeDtypeStruct((N, rows, units), BF16),
        [pltpu.VMEM((units, width), BF16)]
        + [pltpu.VMEM(x.shape, BF16) for x in flat]
        + [pltpu.VMEM((N, rows, units), BF16)],
        [at, w_down] + flat,
        1 + len(flat) + N,
        1,
    )


def weight_grads(chunks, acts, at):
    rows, cols = acts.shape
    units = cols // 2
    width = sum(2 * parts[0][0].shape[1] for parts in chunks)
    flat = [x for parts in chunks for pair in parts for x in pair]

    def body(at_ref, a_ref, *refs):
        x_refs, outs, refs = refs[: len(flat)], refs[len(flat) : len(flat) + 2], refs[len(flat) + 2 :]
        a_buf, x_bufs, out_bufs, sems = refs[0], refs[1:-3], refs[-3:-1], refs[-1]
        copies = Copies(sems)
        first = copies.start(a_ref, a_buf)
        loads = [copies.start(src, dst) for src, dst in zip(x_refs, x_bufs)]
        first.wait()
        stores = []
        for j in range(N):
            lo = 0
            for h in range(len(chunks)):
                for c in range(2):
                    i = (h * N + j) * 2 + c
                    w = x_bufs[i].shape[1]
                    loads[i].wait()
                    grads = dot(x_bufs[i][...], a_buf[...], TN)
                    for o in range(2):
                        out_bufs[o][j, lo : lo + w] = grads[:, o * units : (o + 1) * units].astype(BF16)
                    lo += w
            stores += [copies.start(out_bufs[o].at[j], outs[o].at[other(at_ref, j)]) for o in range(2)]
        for copy in stores:
            copy.wait()

    out = jax.ShapeDtypeStruct((N, width, units), BF16)
    return call(
        body,
        (out, out),
        [pltpu.VMEM((rows, cols), BF16)]
        + [pltpu.VMEM(x.shape, BF16) for x in flat]
        + [pltpu.VMEM(out.shape, BF16)] * 2,
        [at, acts] + flat,
        1 + len(flat) + 2 * N,
        1,
    )


def down_grad(chunks, hiddens, at):
    rows, units = hiddens[0].shape
    width = sum(2 * parts[0][0].shape[1] for parts in chunks)
    flat = [x for parts in chunks for pair in parts for x in pair]

    def body(at_ref, *refs):
        h_refs, x_refs, out, refs = refs[:N], refs[N : N + len(flat)], refs[N + len(flat)], refs[N + len(flat) + 1 :]
        h_buf, x_bufs, out_buf, sems = refs[0], refs[1:-2], refs[-2], refs[-1]
        copies = Copies(sems)
        first = [copies.start(h_refs[j], h_buf.at[j]) for j in range(N)]
        loads = [copies.start(src, dst) for src, dst in zip(x_refs, x_bufs)]
        for copy in first:
            copy.wait()
        lo = 0
        for h in range(len(chunks)):
            for c in range(2):
                total = None
                for j in range(N):
                    i = (h * N + j) * 2 + c
                    loads[i].wait()
                    term = dot(h_buf[(at_ref[0] + j - at_ref[1]) & (N - 1)], x_bufs[i][...], TN)
                    total = term if total is None else total + term
                w = x_bufs[i].shape[1]
                out_buf[:, lo : lo + w] = total
                lo += w
        copies.start(out_buf, out).wait()

    return call(
        body,
        jax.ShapeDtypeStruct((units, width), F32),
        [pltpu.VMEM((N, rows, units), BF16)]
        + [pltpu.VMEM(x.shape, BF16) for x in flat]
        + [pltpu.VMEM((units, width), F32)],
        [at] + list(hiddens) + flat,
        N + len(flat) + 1,
        1,
    )


def input_grads(acts, w_in, at, pieces, adds=None):
    rows, cols = acts.shape
    adds = adds or [[] for _ in pieces]
    flat = [x for group in adds for x in group]

    def body(at_ref, a_ref, w_ref, *refs):
        n = len(pieces)
        add_refs, outs, refs = refs[: len(flat)], refs[len(flat) : len(flat) + n], refs[len(flat) + n :]
        a_buf, w_bufs, add_bufs = refs[0], refs[1 : 1 + n], refs[1 + n : 1 + n + len(flat)]
        out_bufs, sems = refs[1 + n + len(flat) : -1], refs[-1]
        copies = Copies(sems)
        first = copies.start(a_ref, a_buf)
        loads = [copies.start(w_ref.at[other(at_ref, j), pl.ds(lo, w)], b) for (j, lo, w), b in zip(pieces, w_bufs)]
        more = [copies.start(src, dst) for src, dst in zip(add_refs, add_bufs)]
        first.wait()
        stores, k = [], 0
        for i in range(n):
            loads[i].wait()
            total = dot(a_buf[...], w_bufs[i][...], NT)
            for _ in adds[i]:
                more[k].wait()
                total = total + add_bufs[k][...].astype(F32)
                k += 1
            out_bufs[i][...] = total.astype(BF16)
            stores.append(copies.start(out_bufs[i], outs[i]))
        for copy in stores:
            copy.wait()

    outs = tuple(jax.ShapeDtypeStruct((rows, w), BF16) for _, _, w in pieces)
    return call(
        body,
        outs,
        [pltpu.VMEM((rows, cols), BF16)]
        + [pltpu.VMEM((w, cols), BF16) for _, _, w in pieces]
        + [pltpu.VMEM(x.shape, BF16) for x in flat]
        + [pltpu.VMEM(o.shape, BF16) for o in outs],
        [at, acts, w_in] + flat,
        1 + 2 * len(pieces) + len(flat),
        1,
    )


def slots_of(route, experts):
    rows, top = route.shape
    expert_of = route.reshape(rows * top)
    onehot = (expert_of[:, None] == jnp.arange(experts, dtype=jnp.int32)[None, :]).astype(jnp.int32)
    earlier = jnp.cumsum(onehot, axis=0) - onehot
    position = jnp.sum(earlier * onehot, axis=1)
    return route, position.reshape(rows, top)


def per_device(tokens, grad_out, route_ids, combine, gate_weight, up_weight, down_weight):
    rows, width = tokens.shape
    top = route_ids.shape[1]
    groups = lax.axis_size("expert")
    experts = gate_weight.shape[0] * groups
    capacity = min(rows, (5 * top * rows + 4 * experts - 1) // (4 * experts))
    slots = experts * capacity
    piece = (width // 4 + 127) // 128 * 128
    pieces = (piece, width // 2 - piece)
    starts = (0, 2 * piece)
    at = jnp.stack([lax.axis_index("ffn"), lax.axis_index("dp")]).astype(jnp.int32)

    def shift(x, by, axis="ffn"):
        return lax.ppermute(x, axis, [(i, (i + by) % N) for i in range(N)])

    def flip(x):
        return lax.ppermute(
            x, ("dp", "ffn"), [(a * N + b, b * N + a) for a in range(N) for b in range(N)]
        )

    def exchange(x):
        return lax.all_to_all(x, "expert", split_axis=0, concat_axis=0, tiled=True)

    def gather_rows(received):
        own = [received[:, c * capacity : (c + 1) * capacity].reshape(slots, -1) for c in range(2)]
        left = [shift(own[0], 1), None]
        right = [None, shift(own[1], -1)]
        left[1], right[0] = shift(own[1], 1), shift(own[0], -1)
        far = [shift(left[0], 1), shift(right[1], -1)]
        return [own, right, far, left]

    w_in = jnp.concatenate([gate_weight[0], up_weight[0]], axis=1)
    w_in = lax.all_gather(w_in, "dp", axis=0, tiled=False)

    z_local = flip(grad_out)
    routing = flip(jnp.concatenate([route_ids.astype(F32), combine], axis=1))

    slot_index = jnp.arange(2 * slots, dtype=jnp.int32)[:, None]

    def one_hot(route, scale=None):
        expert, place = slots_of(route, experts)
        hits = []
        for c in range(2):
            target = expert * (2 * capacity) + c * capacity + place
            hits.append([slot_index == target[:, k][None, :] for k in range(top)])
        chosen = jnp.concatenate([sum(h.astype(BF16) for h in hit) for hit in hits], axis=1)
        if scale is None:
            return chosen
        weight = sum(
            jnp.sum(jnp.where(hit[k], scale[:, k][None, :], 0.0), axis=1) for hit in hits for k in range(top)
        )
        return chosen, weight[:, None]

    x_place = one_hot(route_ids)
    z_place, z_scale = one_hot(routing[:, :top].astype(jnp.int32), routing[:, top:])

    def stacked(x, h):
        lo, w = starts[h], pieces[h]
        return jnp.concatenate([x[:, lo : lo + w], x[:, lo + w : lo + 2 * w]], axis=0)

    def pack_x(h):
        return dot(x_place, stacked(tokens, h), NN).astype(BF16).reshape(groups, 2 * capacity, -1)

    def pack_z(h):
        packed = dot(z_place, stacked(z_local, h), NN) * z_scale
        return packed.astype(BF16).reshape(groups, 2 * capacity, -1)

    def after(x, parts):
        return lax.optimization_barrier((x, parts[1], parts[3]))[0]

    x_0 = gather_rows(exchange(pack_x(0)))
    z_0 = gather_rows(exchange(pack_z(0)))
    z_1 = gather_rows(exchange(after(pack_z(1), x_0)))
    x_1 = gather_rows(exchange(after(pack_x(1), z_0)))

    partial = hidden_grads((z_0, z_1), down_weight[0], at)
    grads = [partial[0], shift(partial[1], 1, "dp"), shift(partial[2], 2, "dp"), shift(partial[3], 3, "dp")]
    base = project(x_0, w_in, at, starts[0])
    hidden, acts = project(x_1, w_in, at, starts[1], base, grads)

    part_gate, part_up = weight_grads((x_0, x_1), acts, at)
    grad_gate = lax.psum_scatter(part_gate, "dp", scatter_dimension=0, tiled=True).astype(F32)
    grad_up = lax.psum_scatter(part_up, "dp", scatter_dimension=0, tiled=True).astype(F32)

    lead = []
    for h in range(2):
        lo, w = starts[h], pieces[h]
        lead += [(2, lo, w), (2, lo + w, w), (1, lo + w, w), (3, lo, w)]
    lead = input_grads(acts, w_in, at, lead)
    grad_tokens = []
    for h in range(2):
        lo, w = starts[h], pieces[h]
        far_0, far_1, right_1, left_0 = lead[4 * h : 4 * h + 4]
        far_0, far_1 = shift(far_0, 1), shift(far_1, -1)
        right_1, left_0 = shift(right_1, 1), shift(left_0, -1)
        right_0, left_1 = input_grads(acts, w_in, at, [(1, lo, w), (3, lo + w, w)], [[far_0], [far_1]])
        right_0, left_1 = shift(right_0, 1), shift(left_1, -1)
        total = input_grads(acts, w_in, at, [(0, lo, w), (0, lo + w, w)], [[right_0, left_0], [right_1, left_1]])
        total = jnp.concatenate([t.reshape(groups, capacity, w) for t in total], axis=1)
        back = exchange(total).reshape(2 * slots, w)
        back = dot(x_place, back, TN).astype(BF16)
        grad_tokens += [back[:rows], back[rows:]]
    grad_tokens = jnp.concatenate(grad_tokens, axis=1)

    hiddens = [hidden] + [shift(hidden, -j, "dp") for j in range(1, N)]
    grad_down = down_grad((z_0, z_1), hiddens, at)[None]
    return grad_tokens, grad_gate, grad_up, grad_down


def solution(mesh):
    return jax.shard_map(
        per_device,
        mesh=mesh,
        in_specs=(
            P(("dp", "expert"), "ffn"),
            P(("dp", "expert"), "ffn"),
            P(("dp", "expert"), None),
            P(("dp", "expert"), None),
            P("expert", "dp", "ffn"),
            P("expert", "dp", "ffn"),
            P("expert", "ffn", "dp"),
        ),
        out_specs=(
            P(("dp", "expert"), "ffn"),
            P("expert", "dp", "ffn"),
            P("expert", "dp", "ffn"),
            P("expert", "ffn", "dp"),
        ),
        check_vma=False,
    )
```

```python
import jax
import jax.numpy as jnp
from jax import lax
from jax.experimental import pallas as pl
from jax.experimental.pallas import tpu as pltpu
from jax.sharding import PartitionSpec as P


F32 = jnp.float32
BF16 = jnp.bfloat16
N = 4
ANY = pl.BlockSpec(memory_space=pl.ANY)
SMEM = pl.BlockSpec(memory_space=pltpu.SMEM)


def dot(a, b, contract):
    return lax.dot_general(a, b, (contract, ((), ())), preferred_element_type=F32)


NN, NT, TN = ((1,), (0,)), ((1,), (1,)), ((0,), (0,))


def call(body, outs, scratch, args, copies):
    return pl.pallas_call(
        body,
        out_shape=outs,
        in_specs=[SMEM] + [ANY] * (len(args) - 1),
        out_specs=jax.tree.map(lambda _: ANY, outs),
        scratch_shapes=list(scratch) + [pltpu.SemaphoreType.DMA((copies,))],
    )(*args)


def start(src, dst, sem):
    copy = pltpu.make_async_copy(src, dst, sem)
    copy.start()
    return copy


def wrap(x):
    return x & (N - 1)


def vmem(*shape, dtype=BF16):
    return pltpu.VMEM(shape, dtype)


def project(parts, w_in, at, offset, base=None, grads=None):
    _, rows, width = parts[0].shape
    cols = w_in.shape[2]
    units = cols // 2
    last = base is not None

    def body(at_ref, w_ref, *refs):
        x_refs, refs = refs[:N], refs[N:]
        if last:
            (base_ref, grad_ref), refs = refs[:2], refs[2:]
            out_h, out_a, w_buf, x_buf, total, h_buf, a_buf, grad_buf, sems = refs
        else:
            out, w_buf, x_buf, total, sems = refs
        for j in range(N):
            start(w_ref.at[wrap(at_ref[0] + j), pl.ds(offset, 2 * width)], w_buf.at[j], sems.at[j])
            start(x_refs[j], x_buf.at[j], sems.at[N + j])
        if last:
            first = start(base_ref, total, sems.at[2 * N])
            second = start(grad_ref, grad_buf, sems.at[2 * N + 1])
            first.wait()
        else:
            total[...] = jnp.zeros_like(total)

        def step(j, carry):
            pltpu.make_async_copy(w_ref.at[0, pl.ds(offset, 2 * width)], w_buf.at[j], sems.at[j]).wait()
            pltpu.make_async_copy(x_refs[0], x_buf.at[j], sems.at[N + j]).wait()
            total[...] += dot(x_buf[j, 0], w_buf[j, :width], NN) + dot(x_buf[j, 1], w_buf[j, width:], NN)
            return carry

        lax.fori_loop(0, N, step, 0)
        if last:
            second.wait()
            grad = sum(grad_buf[j].astype(F32) for j in range(N))
            gate, up = total[:, :units], total[:, units:]
            sig = jax.nn.sigmoid(gate)
            h_buf[...] = (gate * sig * up).astype(BF16)
            a_buf[:, :units] = (grad * up * sig * (1.0 + gate * (1.0 - sig))).astype(BF16)
            a_buf[:, units:] = (grad * gate * sig).astype(BF16)
            stores = [start(h_buf, out_h, sems.at[0]), start(a_buf, out_a, sems.at[1])]
        else:
            stores = [start(total, out, sems.at[0])]
        for copy in stores:
            copy.wait()

    scratch = [vmem(N, 2 * width, cols), vmem(N, 2, rows, width), vmem(rows, cols, dtype=F32)]
    if not last:
        return call(body, jax.ShapeDtypeStruct((rows, cols), F32), scratch, [at, w_in] + parts, 2 * N)
    outs = (jax.ShapeDtypeStruct((rows, units), BF16), jax.ShapeDtypeStruct((rows, cols), BF16))
    scratch += [vmem(rows, units), vmem(rows, cols), vmem(N, rows, units)]
    return call(body, outs, scratch, [at, w_in] + parts + [base, grads], 2 * N + 2)


def fetch(chunks, x_refs, x_bufs, sems, base):
    for j in range(N):
        for h in range(len(chunks)):
            start(x_refs[h * N + j], x_bufs[h].at[j], sems.at[base + h * N + j])


def arrived(x_refs, x_bufs, sems, base, h, j):
    pltpu.make_async_copy(x_refs[h * N], x_bufs[h].at[j], sems.at[base + h * N + j]).wait()


def flat(chunks):
    return [x for parts in chunks for x in parts]


def buffers(chunks):
    return [vmem(N, *parts[0].shape) for parts in chunks]


def hidden_grads(chunks, w_down, at):
    rows = chunks[0][0].shape[1]
    units, width = w_down.shape
    count = len(chunks)

    def body(at_ref, w_ref, *refs):
        x_refs, (out, w_buf, *x_bufs, out_buf, sems) = refs[: count * N], refs[count * N :]
        first = start(w_ref, w_buf, sems.at[0])
        fetch(chunks, x_refs, x_bufs, sems, 1 + N)
        first.wait()

        def step(j, carry):
            total, lo = None, 0
            for h in range(count):
                w = x_bufs[h].shape[3]
                arrived(x_refs, x_bufs, sems, 1 + N, h, j)
                for c in range(2):
                    term = dot(x_bufs[h][j, c], w_buf[:, lo : lo + w], NT)
                    total = term if total is None else total + term
                    lo += w
            out_buf[j] = total.astype(BF16)
            start(out_buf.at[j], out.at[wrap(at_ref[0] + j)], sems.at[1 + j])
            return carry

        lax.fori_loop(0, N, step, 0)
        for j in range(N):
            pltpu.make_async_copy(out_buf.at[j], out.at[0], sems.at[1 + j]).wait()

    scratch = [vmem(units, width)] + buffers(chunks) + [vmem(N, rows, units)]
    out = jax.ShapeDtypeStruct((N, rows, units), BF16)
    return call(body, out, scratch, [at, w_down] + flat(chunks), 1 + N + count * N)


def weight_grad(chunks, acts, at, lo_col):
    rows, cols = acts.shape
    units = cols // 2
    width = sum(2 * parts[0].shape[2] for parts in chunks)
    count = len(chunks)

    def body(at_ref, a_ref, *refs):
        x_refs, (out, a_buf, *x_bufs, out_buf, sems) = refs[: count * N], refs[count * N :]
        first = start(a_ref, a_buf, sems.at[0])
        fetch(chunks, x_refs, x_bufs, sems, 1 + N)
        first.wait()

        def step(j, carry):
            lo = 0
            for h in range(count):
                w = x_bufs[h].shape[3]
                arrived(x_refs, x_bufs, sems, 1 + N, h, j)
                for c in range(2):
                    grads = dot(x_bufs[h][j, c], a_buf[:, lo_col : lo_col + units], TN)
                    out_buf[j, lo : lo + w] = grads.astype(BF16)
                    lo += w
            start(out_buf.at[j], out.at[wrap(at_ref[0] + j)], sems.at[1 + j])
            return carry

        lax.fori_loop(0, N, step, 0)
        for j in range(N):
            pltpu.make_async_copy(out_buf.at[j], out.at[0], sems.at[1 + j]).wait()

    scratch = [vmem(rows, cols)] + buffers(chunks) + [vmem(N, width, units)]
    out = jax.ShapeDtypeStruct((N, width, units), BF16)
    return call(body, out, scratch, [at, acts] + flat(chunks), 1 + N + count * N)


def down_grad(chunks, hidden, at):
    _, rows, units = hidden.shape
    width = sum(2 * parts[0].shape[2] for parts in chunks)
    count = len(chunks)

    def body(at_ref, h_ref, *refs):
        x_refs, (out, h_buf, *x_bufs, out_buf, sems) = refs[: count * N], refs[count * N :]
        first = start(h_ref, h_buf, sems.at[0])
        fetch(chunks, x_refs, x_bufs, sems, 1)
        out_buf[...] = jnp.zeros_like(out_buf)
        first.wait()

        def step(j, carry):
            lo = 0
            for h in range(count):
                w = x_bufs[h].shape[3]
                arrived(x_refs, x_bufs, sems, 1, h, j)
                for c in range(2):
                    out_buf[:, lo : lo + w] += dot(h_buf[wrap(at_ref[0] + j)], x_bufs[h][j, c], TN)
                    lo += w
            return carry

        lax.fori_loop(0, N, step, 0)
        start(out_buf, out, sems.at[0]).wait()

    scratch = [vmem(N, rows, units)] + buffers(chunks) + [vmem(units, width, dtype=F32)]
    out = jax.ShapeDtypeStruct((units, width), F32)
    return call(body, out, scratch, [at, hidden] + flat(chunks), 1 + count * N)


def input_partials(acts, w_in, at, offset, width):
    rows, cols = acts.shape

    def body(at_ref, a_ref, w_ref, *refs):
        outs, (a_buf, w_buf, out_buf, sems) = refs[: N - 1], refs[N - 1 :]
        first = start(a_ref, a_buf, sems.at[0])
        for j in range(1, N):
            start(w_ref.at[wrap(at_ref[0] + j), pl.ds(offset, 2 * width)], w_buf.at[j - 1], sems.at[j])
        first.wait()

        def step(j, carry):
            pltpu.make_async_copy(w_ref.at[0, pl.ds(offset, 2 * width)], w_buf.at[j], sems.at[1 + j]).wait()
            for c in range(2):
                out_buf[j, c] = dot(a_buf[...], w_buf[j, c * width : (c + 1) * width], NT).astype(BF16)
            return carry

        lax.fori_loop(0, N - 1, step, 0)
        stores = [start(out_buf.at[j], outs[j], sems.at[j]) for j in range(N - 1)]
        for copy in stores:
            copy.wait()

    outs = (jax.ShapeDtypeStruct((2, rows, width), BF16),) * (N - 1)
    scratch = [vmem(rows, cols), vmem(N - 1, 2 * width, cols), vmem(N - 1, 2, rows, width)]
    return call(body, outs, scratch, [at, acts, w_in], N)


def input_totals(acts, w_in, at, offset, received, order):
    rows, cols = acts.shape
    _, _, width = received[0].shape

    def body(at_ref, a_ref, w_ref, order_ref, *refs):
        r_refs, (out, a_buf, w_buf, o_buf, r_buf, t_buf, out_buf, sems) = refs[: N - 1], refs[N - 1 :]
        copies = [
            start(a_ref, a_buf, sems.at[0]),
            start(w_ref.at[at_ref[0], pl.ds(offset, 2 * width)], w_buf, sems.at[1]),
            start(order_ref, o_buf, sems.at[2]),
        ]
        copies += [start(r_refs[j], r_buf.at[j], sems.at[3 + j]) for j in range(N - 1)]
        for copy in copies:
            copy.wait()
        for c in range(2):
            total = dot(a_buf[...], w_buf[c * width : (c + 1) * width], NT)
            for j in range(N - 1):
                total = total + r_buf[j, c].astype(F32)
            t_buf[c * rows : (c + 1) * rows] = total.astype(BF16)

        def step(i, carry):
            block = pl.ds(i * (rows // 2), rows // 2)
            out_buf[block] = dot(o_buf[block], t_buf[...], NN).astype(BF16)
            return carry

        lax.fori_loop(0, 4, step, 0)
        start(out_buf, out, sems.at[0]).wait()

    scratch = [vmem(rows, cols), vmem(2 * width, cols), vmem(2 * rows, 2 * rows), vmem(N - 1, 2, rows, width)]
    scratch += [vmem(2 * rows, width), vmem(2 * rows, width)]
    out = jax.ShapeDtypeStruct((2 * rows, width), BF16)
    return call(body, out, scratch, [at, acts, w_in, order] + list(received), 3 + N - 1)


def slots_of(route, experts, stride):
    rows, top = route.shape
    expert_of = route.reshape(rows * top)
    onehot = (expert_of[:, None] == jnp.arange(experts, dtype=jnp.int32)[None, :]).astype(jnp.int32)
    earlier = jnp.cumsum(onehot, axis=0) - onehot
    position = jnp.sum(earlier * onehot, axis=1)
    return (expert_of * stride + position).reshape(rows, top)


def per_device(tokens, grad_out, route_ids, combine, gate_weight, up_weight, down_weight):
    rows, width = tokens.shape
    top = route_ids.shape[1]
    groups = lax.axis_size("expert")
    experts = gate_weight.shape[0] * groups
    capacity = min(rows, (5 * top * rows + 4 * experts - 1) // (4 * experts))
    slots = experts * capacity
    piece = (width // 4 + 127) // 128 * 128
    pieces = (piece, width // 2 - piece)
    starts = (0, 2 * piece)
    at = lax.axis_index("ffn").astype(jnp.int32)[None]

    def shift(x, by):
        return lax.ppermute(x, "ffn", [(i, (i + by) % N) for i in range(N)])

    def flip(x):
        return lax.ppermute(
            x, ("dp", "ffn"), [(a * N + b, b * N + a) for a in range(N) for b in range(N)]
        )

    def exchange(x):
        return lax.all_to_all(x, "expert", split_axis=0, concat_axis=0, tiled=True)

    def gather_rows(packed):
        received = exchange(packed)
        own = dot(order, received.reshape(2 * slots, -1), NN).astype(BF16).reshape(2, slots, -1)
        return [own, shift(own, -1), shift(own, 2), shift(own, 1)]

    z_local = flip(grad_out)

    to = jnp.arange(2 * slots, dtype=jnp.int32)
    to = to % slots // capacity * (2 * capacity) + to // slots * capacity + to % capacity
    order = (to[:, None] == jnp.arange(2 * slots, dtype=jnp.int32)[None, :]).astype(BF16)
    order_back = (jnp.arange(2 * slots, dtype=jnp.int32)[:, None] == to[None, :]).astype(BF16)

    w_in = jnp.concatenate([gate_weight[0], up_weight[0]], axis=1)
    w_in = lax.all_gather(w_in, "dp", axis=0, tiled=False)

    slot_index = jnp.arange(2 * slots, dtype=jnp.int32)[:, None]

    def hits_of(slot):
        return [[slot_index == (slot[:, k] + c * capacity)[None, :] for k in range(top)] for c in range(2)]

    def one_hot(hits):
        return jnp.concatenate([sum(h.astype(BF16) for h in hit) for hit in hits], axis=1)

    slot = slots_of(route_ids, experts, 2 * capacity)
    x_place = one_hot(hits_of(slot))
    routing = flip(jnp.concatenate([slot.astype(F32), combine], axis=1))
    z_hits = hits_of(routing[:, :top].astype(jnp.int32))
    z_place = one_hot(z_hits)
    z_scale = jnp.zeros((), F32)
    for hit in z_hits:
        for k in range(top):
            z_scale = jnp.where(hit[k], routing[:, top + k][None, :], z_scale)
    z_scale = jnp.sum(z_scale, axis=1)[:, None]

    def stacked(x, h):
        lo, w = starts[h], pieces[h]
        return jnp.concatenate([x[:, lo : lo + w], x[:, lo + w : lo + 2 * w]], axis=0)

    def pack_x(h):
        return dot(x_place, stacked(tokens, h), NN).astype(BF16).reshape(groups, 2 * capacity, -1)

    def pack_z(h):
        packed = dot(z_place, stacked(z_local, h), NN) * z_scale
        return packed.astype(BF16).reshape(groups, 2 * capacity, -1)

    x_0 = gather_rows(pack_x(0))
    z_0 = gather_rows(pack_z(0))
    z_1 = gather_rows(pack_z(1))
    x_1 = gather_rows(pack_x(1))

    partial = hidden_grads((z_0, z_1), down_weight[0], at)
    grads = lax.all_to_all(partial, "dp", split_axis=0, concat_axis=0, tiled=True)
    base = project(x_0, w_in, at, starts[0])
    hidden, acts = project(x_1, w_in, at, starts[1], base, grads)

    part_gate = weight_grad((x_0, x_1), acts, at, 0)
    grad_gate = lax.psum_scatter(part_gate, "dp", scatter_dimension=0, tiled=True)
    grad_gate = grad_gate.astype(F32)
    leads = [input_partials(acts, w_in, at, starts[h], pieces[h]) for h in range(2)]
    received = []
    for h in range(2):
        received.append([shift(leads[h][j - 1], j) for j in range(1, N)])
    part_up = weight_grad((x_0, x_1), acts, at, gate_weight.shape[2])
    grad_up = lax.psum_scatter(part_up, "dp", scatter_dimension=0, tiled=True).astype(F32)

    grad_tokens = []
    for h in range(2):
        total = input_totals(acts, w_in, at, starts[h], received[h], order_back)
        back = exchange(total.reshape(groups, 2 * capacity, -1))
        back = back.reshape(2 * slots, -1)
        back = dot(x_place, back, TN).astype(BF16)
        grad_tokens += [back[:rows], back[rows:]]
    grad_tokens = jnp.concatenate(grad_tokens, axis=1)

    hidden = lax.optimization_barrier((hidden, leads[1][0]))[0]
    hidden_all = lax.all_gather(hidden, "dp", axis=0, tiled=False)
    grad_down = down_grad((z_0, z_1), hidden_all, at)[None]
    return grad_tokens, grad_gate, grad_up, grad_down


def solution(mesh):
    return jax.shard_map(
        per_device,
        mesh=mesh,
        in_specs=(
            P(("dp", "expert"), "ffn"),
            P(("dp", "expert"), "ffn"),
            P(("dp", "expert"), None),
            P(("dp", "expert"), None),
            P("expert", "dp", "ffn"),
            P("expert", "dp", "ffn"),
            P("expert", "ffn", "dp"),
        ),
        out_specs=(
            P(("dp", "expert"), "ffn"),
            P("expert", "dp", "ffn"),
            P("expert", "dp", "ffn"),
            P("expert", "ffn", "dp"),
        ),
        check_vma=False,
    )
```

```python
import jax
import jax.numpy as jnp
from jax import lax
from jax.experimental import pallas as pl
from jax.experimental.pallas import tpu as pltpu
from jax.sharding import PartitionSpec as P


F32 = jnp.float32
BF16 = jnp.bfloat16
N = 4
ANY = pl.BlockSpec(memory_space=pl.ANY)
SMEM = pl.BlockSpec(memory_space=pltpu.SMEM)


def dot(a, b, contract):
    return lax.dot_general(a, b, (contract, ((), ())), preferred_element_type=F32)


NN, NT, TN = ((1,), (0,)), ((1,), (1,)), ((0,), (0,))


def call(body, outs, scratch, args, copies):
    return pl.pallas_call(
        body,
        out_shape=outs,
        in_specs=[SMEM] + [ANY] * (len(args) - 1),
        out_specs=jax.tree.map(lambda _: ANY, outs),
        scratch_shapes=list(scratch) + [pltpu.SemaphoreType.DMA((copies,))],
    )(*args)


def start(src, dst, sem):
    copy = pltpu.make_async_copy(src, dst, sem)
    copy.start()
    return copy


def wrap(x):
    return x & (N - 1)


def vmem(*shape, dtype=BF16):
    return pltpu.VMEM(shape, dtype)


def project(parts, w_in, at, offset, base=None, grads=None):
    _, rows, width = parts[0].shape
    cols = w_in.shape[2]
    units = cols // 2
    last = base is not None

    def body(at_ref, w_ref, *refs):
        x_refs, refs = refs[:N], refs[N:]
        if last:
            (base_ref, grad_ref), refs = refs[:2], refs[2:]
            out_h, out_a, w_buf, x_buf, total, h_buf, a_buf, grad_buf, sems = refs
        else:
            out, w_buf, x_buf, total, sems = refs
        for j in range(N):
            start(w_ref.at[wrap(at_ref[0] + j), pl.ds(offset, 2 * width)], w_buf.at[j], sems.at[j])
            start(x_refs[j], x_buf.at[j], sems.at[N + j])
        if last:
            first = start(base_ref, total, sems.at[2 * N])
            second = start(grad_ref, grad_buf, sems.at[2 * N + 1])
            first.wait()
        else:
            total[...] = jnp.zeros_like(total)

        def step(j, carry):
            pltpu.make_async_copy(w_ref.at[0, pl.ds(offset, 2 * width)], w_buf.at[j], sems.at[j]).wait()
            pltpu.make_async_copy(x_refs[0], x_buf.at[j], sems.at[N + j]).wait()
            total[...] += dot(x_buf[j, 0], w_buf[j, :width], NN) + dot(x_buf[j, 1], w_buf[j, width:], NN)
            return carry

        lax.fori_loop(0, N, step, 0)
        if last:
            second.wait()
            grad = sum(grad_buf[j].astype(F32) for j in range(N))
            gate, up = total[:, :units], total[:, units:]
            sig = jax.nn.sigmoid(gate)
            h_buf[...] = (gate * sig * up).astype(BF16)
            a_buf[:, :units] = (grad * up * sig * (1.0 + gate * (1.0 - sig))).astype(BF16)
            a_buf[:, units:] = (grad * gate * sig).astype(BF16)
            stores = [start(h_buf, out_h, sems.at[0]), start(a_buf, out_a, sems.at[1])]
        else:
            stores = [start(total, out, sems.at[0])]
        for copy in stores:
            copy.wait()

    scratch = [vmem(N, 2 * width, cols), vmem(N, 2, rows, width), vmem(rows, cols, dtype=F32)]
    if not last:
        return call(body, jax.ShapeDtypeStruct((rows, cols), F32), scratch, [at, w_in] + parts, 2 * N)
    outs = (jax.ShapeDtypeStruct((rows, units), BF16), jax.ShapeDtypeStruct((rows, cols), BF16))
    scratch += [vmem(rows, units), vmem(rows, cols), vmem(N, rows, units)]
    return call(body, outs, scratch, [at, w_in] + parts + [base, grads], 2 * N + 2)


def fetch(chunks, x_refs, x_bufs, sems, base):
    for j in range(N):
        for h in range(len(chunks)):
            start(x_refs[h * N + j], x_bufs[h].at[j], sems.at[base + h * N + j])


def arrived(x_refs, x_bufs, sems, base, h, j):
    pltpu.make_async_copy(x_refs[h * N], x_bufs[h].at[j], sems.at[base + h * N + j]).wait()


def flat(chunks):
    return [x for parts in chunks for x in parts]


def buffers(chunks):
    return [vmem(N, *parts[0].shape) for parts in chunks]


def hidden_grads(chunks, w_down, at):
    rows = chunks[0][0].shape[1]
    units, width = w_down.shape
    count = len(chunks)

    def body(at_ref, w_ref, *refs):
        x_refs, (out, w_buf, *x_bufs, out_buf, sems) = refs[: count * N], refs[count * N :]
        first = start(w_ref, w_buf, sems.at[0])
        fetch(chunks, x_refs, x_bufs, sems, 1 + N)
        first.wait()

        def step(j, carry):
            total, lo = None, 0
            for h in range(count):
                w = x_bufs[h].shape[3]
                arrived(x_refs, x_bufs, sems, 1 + N, h, j)
                for c in range(2):
                    term = dot(x_bufs[h][j, c], w_buf[:, lo : lo + w], NT)
                    total = term if total is None else total + term
                    lo += w
            out_buf[j] = total.astype(BF16)
            start(out_buf.at[j], out.at[wrap(at_ref[0] + j)], sems.at[1 + j])
            return carry

        lax.fori_loop(0, N, step, 0)
        for j in range(N):
            pltpu.make_async_copy(out_buf.at[j], out.at[0], sems.at[1 + j]).wait()

    scratch = [vmem(units, width)] + buffers(chunks) + [vmem(N, rows, units)]
    out = jax.ShapeDtypeStruct((N, rows, units), BF16)
    return call(body, out, scratch, [at, w_down] + flat(chunks), 1 + N + count * N)


def weight_grad(chunks, acts, at, lo_col):
    rows, cols = acts.shape
    units = cols // 2
    width = sum(2 * parts[0].shape[2] for parts in chunks)
    count = len(chunks)

    def body(at_ref, a_ref, *refs):
        x_refs, (out, a_buf, *x_bufs, out_buf, sems) = refs[: count * N], refs[count * N :]
        first = start(a_ref, a_buf, sems.at[0])
        fetch(chunks, x_refs, x_bufs, sems, 1 + N)
        first.wait()

        def step(j, carry):
            lo = 0
            for h in range(count):
                w = x_bufs[h].shape[3]
                arrived(x_refs, x_bufs, sems, 1 + N, h, j)
                for c in range(2):
                    grads = dot(x_bufs[h][j, c], a_buf[:, lo_col : lo_col + units], TN)
                    out_buf[j, lo : lo + w] = grads.astype(BF16)
                    lo += w
            start(out_buf.at[j], out.at[wrap(at_ref[0] + j)], sems.at[1 + j])
            return carry

        lax.fori_loop(0, N, step, 0)
        for j in range(N):
            pltpu.make_async_copy(out_buf.at[j], out.at[0], sems.at[1 + j]).wait()

    scratch = [vmem(rows, cols)] + buffers(chunks) + [vmem(N, width, units)]
    out = jax.ShapeDtypeStruct((N, width, units), BF16)
    return call(body, out, scratch, [at, acts] + flat(chunks), 1 + N + count * N)


def down_grad(chunks, hidden, at):
    _, rows, units = hidden.shape
    width = sum(2 * parts[0].shape[2] for parts in chunks)
    count = len(chunks)

    def body(at_ref, h_ref, *refs):
        x_refs, (out, h_buf, *x_bufs, out_buf, sems) = refs[: count * N], refs[count * N :]
        first = start(h_ref, h_buf, sems.at[0])
        fetch(chunks, x_refs, x_bufs, sems, 1)
        out_buf[...] = jnp.zeros_like(out_buf)
        first.wait()

        def step(j, carry):
            lo = 0
            for h in range(count):
                w = x_bufs[h].shape[3]
                arrived(x_refs, x_bufs, sems, 1, h, j)
                for c in range(2):
                    out_buf[:, lo : lo + w] += dot(h_buf[wrap(at_ref[0] + j)], x_bufs[h][j, c], TN)
                    lo += w
            return carry

        lax.fori_loop(0, N, step, 0)
        start(out_buf, out, sems.at[0]).wait()

    scratch = [vmem(N, rows, units)] + buffers(chunks) + [vmem(units, width, dtype=F32)]
    out = jax.ShapeDtypeStruct((units, width), F32)
    return call(body, out, scratch, [at, hidden] + flat(chunks), 1 + count * N)


def input_partials(acts, w_in, at, offset, width):
    rows, cols = acts.shape

    def body(at_ref, a_ref, w_ref, *refs):
        outs, (a_buf, w_buf, out_buf, sems) = refs[: N - 1], refs[N - 1 :]
        first = start(a_ref, a_buf, sems.at[0])
        for j in range(1, N):
            start(w_ref.at[wrap(at_ref[0] + j), pl.ds(offset, 2 * width)], w_buf.at[j - 1], sems.at[j])
        first.wait()

        def step(j, carry):
            pltpu.make_async_copy(w_ref.at[0, pl.ds(offset, 2 * width)], w_buf.at[j], sems.at[1 + j]).wait()
            for c in range(2):
                out_buf[j, c] = dot(a_buf[...], w_buf[j, c * width : (c + 1) * width], NT).astype(BF16)
            return carry

        lax.fori_loop(0, N - 1, step, 0)
        stores = [start(out_buf.at[j], outs[j], sems.at[j]) for j in range(N - 1)]
        for copy in stores:
            copy.wait()

    outs = (jax.ShapeDtypeStruct((2, rows, width), BF16),) * (N - 1)
    scratch = [vmem(rows, cols), vmem(N - 1, 2 * width, cols), vmem(N - 1, 2, rows, width)]
    return call(body, outs, scratch, [at, acts, w_in], N)


def input_totals(acts, w_in, at, offset, received, order):
    rows, cols = acts.shape
    _, _, width = received[0].shape

    def body(at_ref, a_ref, w_ref, order_ref, *refs):
        r_refs, (out, a_buf, w_buf, o_buf, r_buf, t_buf, out_buf, sems) = refs[: N - 1], refs[N - 1 :]
        copies = [
            start(a_ref, a_buf, sems.at[0]),
            start(w_ref.at[at_ref[0], pl.ds(offset, 2 * width)], w_buf, sems.at[1]),
            start(order_ref, o_buf, sems.at[2]),
        ]
        copies += [start(r_refs[j], r_buf.at[j], sems.at[3 + j]) for j in range(N - 1)]
        for copy in copies:
            copy.wait()
        for c in range(2):
            total = dot(a_buf[...], w_buf[c * width : (c + 1) * width], NT)
            for j in range(N - 1):
                total = total + r_buf[j, c].astype(F32)
            t_buf[c * rows : (c + 1) * rows] = total.astype(BF16)

        def step(i, carry):
            block = pl.ds(i * (rows // 2), rows // 2)
            out_buf[block] = dot(o_buf[block], t_buf[...], NN).astype(BF16)
            return carry

        lax.fori_loop(0, 4, step, 0)
        start(out_buf, out, sems.at[0]).wait()

    scratch = [vmem(rows, cols), vmem(2 * width, cols), vmem(2 * rows, 2 * rows), vmem(N - 1, 2, rows, width)]
    scratch += [vmem(2 * rows, width), vmem(2 * rows, width)]
    out = jax.ShapeDtypeStruct((2 * rows, width), BF16)
    return call(body, out, scratch, [at, acts, w_in, order] + list(received), 3 + N - 1)


def slots_of(route, experts, stride):
    rows, top = route.shape
    expert_of = route.reshape(rows * top)
    onehot = (expert_of[:, None] == jnp.arange(experts, dtype=jnp.int32)[None, :]).astype(jnp.int32)
    earlier = jnp.cumsum(onehot, axis=0) - onehot
    position = jnp.sum(earlier * onehot, axis=1)
    return (expert_of * stride + position).reshape(rows, top)


def per_device(tokens, grad_out, route_ids, combine, gate_weight, up_weight, down_weight):
    rows, width = tokens.shape
    top = route_ids.shape[1]
    groups = lax.axis_size("expert")
    experts = gate_weight.shape[0] * groups
    capacity = min(rows, (5 * top * rows + 4 * experts - 1) // (4 * experts))
    slots = experts * capacity
    piece = (width // 4 + 127) // 128 * 128
    small = width // 2 - piece
    pieces, starts = (small, piece), (0, 2 * small)
    z_pieces, z_starts = (piece, small), (0, 2 * piece)
    at = lax.axis_index("ffn").astype(jnp.int32)[None]

    def shift(x, by):
        return lax.ppermute(x, "ffn", [(i, (i + by) % N) for i in range(N)])

    def flip(x):
        return lax.ppermute(
            x, ("dp", "ffn"), [(a * N + b, b * N + a) for a in range(N) for b in range(N)]
        )

    def exchange(x):
        return lax.all_to_all(x, "expert", split_axis=0, concat_axis=0, tiled=True)

    def gather_rows(packed):
        received = exchange(packed)
        own = dot(order, received.reshape(2 * slots, -1), NN).astype(BF16).reshape(2, slots, -1)
        return [own, shift(own, -1), shift(own, 2), shift(own, 1)]

    z_local = flip(grad_out)

    to = jnp.arange(2 * slots, dtype=jnp.int32)
    to = to % slots // capacity * (2 * capacity) + to // slots * capacity + to % capacity
    order = (to[:, None] == jnp.arange(2 * slots, dtype=jnp.int32)[None, :]).astype(BF16)
    order_back = (jnp.arange(2 * slots, dtype=jnp.int32)[:, None] == to[None, :]).astype(BF16)

    w_in = jnp.concatenate([gate_weight[0], up_weight[0]], axis=1)
    w_in = lax.all_gather(w_in, "dp", axis=0, tiled=False)

    slot_index = jnp.arange(2 * slots, dtype=jnp.int32)[:, None]

    def hits_of(slot):
        return [[slot_index == (slot[:, k] + c * capacity)[None, :] for k in range(top)] for c in range(2)]

    def one_hot(hits):
        return jnp.concatenate([sum(h.astype(BF16) for h in hit) for hit in hits], axis=1)

    slot = slots_of(route_ids, experts, 2 * capacity)
    x_place = one_hot(hits_of(slot))
    routing = flip(jnp.concatenate([slot.astype(F32), combine], axis=1))
    z_hits = hits_of(routing[:, :top].astype(jnp.int32))
    z_place = one_hot(z_hits)
    z_scale = jnp.zeros((), F32)
    for hit in z_hits:
        for k in range(top):
            z_scale = jnp.where(hit[k], routing[:, top + k][None, :], z_scale)
    z_scale = jnp.sum(z_scale, axis=1)[:, None]

    def stacked(x, lo, w):
        return jnp.concatenate([x[:, lo : lo + w], x[:, lo + w : lo + 2 * w]], axis=0)

    def pack_x(h):
        return dot(x_place, stacked(tokens, starts[h], pieces[h]), NN).astype(BF16).reshape(groups, 2 * capacity, -1)

    def pack_z(h):
        packed = dot(z_place, stacked(z_local, z_starts[h], z_pieces[h]), NN) * z_scale
        return packed.astype(BF16).reshape(groups, 2 * capacity, -1)

    x_0 = gather_rows(pack_x(0))
    z_0 = gather_rows(pack_z(0))
    z_1 = gather_rows(pack_z(1))
    x_1 = gather_rows(pack_x(1))

    partial = hidden_grads((z_0, z_1), down_weight[0], at)
    grads = lax.all_to_all(partial, "dp", split_axis=0, concat_axis=0, tiled=True)
    base = project(x_0, w_in, at, starts[0])
    hidden, acts = project(x_1, w_in, at, starts[1], base, grads)

    part_gate = weight_grad((x_0, x_1), acts, at, 0)
    grad_gate = lax.psum_scatter(part_gate, "dp", scatter_dimension=0, tiled=True)
    grad_gate = grad_gate.astype(F32)
    leads = []
    for h in range(2):
        leads.append(input_partials(acts, w_in, at, starts[h], pieces[h]))
    received = []
    for h in range(2):
        received.append([shift(leads[h][j - 1], j) for j in range(1, N)])
    part_up = weight_grad((x_0, x_1), acts, at, gate_weight.shape[2])
    grad_up = lax.psum_scatter(part_up, "dp", scatter_dimension=0, tiled=True).astype(F32)

    grad_tokens = []
    hidden_all = lax.all_gather(hidden, "dp", axis=0, tiled=False)
    received[1] = lax.optimization_barrier((received[1], hidden_all))[0]
    for h in range(2):
        total = input_totals(acts, w_in, at, starts[h], received[h], order_back)
        back = exchange(total.reshape(groups, 2 * capacity, -1))
        back = back.reshape(2 * slots, -1)
        back = dot(x_place, back, TN).astype(BF16)
        grad_tokens += [back[:rows], back[rows:]]
    grad_tokens = jnp.concatenate(grad_tokens, axis=1)

    grad_down = down_grad((z_0, z_1), hidden_all, at)[None]
    return grad_tokens, grad_gate, grad_up, grad_down


def solution(mesh):
    return jax.shard_map(
        per_device,
        mesh=mesh,
        in_specs=(
            P(("dp", "expert"), "ffn"),
            P(("dp", "expert"), "ffn"),
            P(("dp", "expert"), None),
            P(("dp", "expert"), None),
            P("expert", "dp", "ffn"),
            P("expert", "dp", "ffn"),
            P("expert", "ffn", "dp"),
        ),
        out_specs=(
            P(("dp", "expert"), "ffn"),
            P("expert", "dp", "ffn"),
            P("expert", "dp", "ffn"),
            P("expert", "ffn", "dp"),
        ),
        check_vma=False,
    )
```

```python
import jax
import jax.numpy as jnp
from jax import lax
from jax.experimental import pallas as pl
from jax.experimental.pallas import tpu as pltpu
from jax.sharding import PartitionSpec as P


F32 = jnp.float32
BF16 = jnp.bfloat16
N = 4
ANY = pl.BlockSpec(memory_space=pl.ANY)
SMEM = pl.BlockSpec(memory_space=pltpu.SMEM)


def dot(a, b, contract):
    return lax.dot_general(a, b, (contract, ((), ())), preferred_element_type=F32)


NN, NT, TN = ((1,), (0,)), ((1,), (1,)), ((0,), (0,))


def call(body, outs, scratch, args, copies):
    return pl.pallas_call(
        body,
        out_shape=outs,
        in_specs=[SMEM] + [ANY] * (len(args) - 1),
        out_specs=jax.tree.map(lambda _: ANY, outs),
        scratch_shapes=list(scratch) + [pltpu.SemaphoreType.DMA((copies,))],
    )(*args)


def start(src, dst, sem):
    copy = pltpu.make_async_copy(src, dst, sem)
    copy.start()
    return copy


def place(part, buf, sem):
    if len(part) == 1:
        start(part[0], buf, sem)
    else:
        for c in range(2):
            start(part[c], buf.at[c], sem)


def grouped(refs):
    return [[refs[0]], [refs[1]], [refs[2], refs[3]], [refs[4]]]


PER = N + 1


def vmem(*shape, dtype=BF16):
    return pltpu.VMEM(shape, dtype)


def project(parts, w_in, at, offset, base=None, grads=None):
    _, rows, width = parts[0].shape
    cols = w_in.shape[2]
    units = cols // 2
    last = base is not None

    def body(at_ref, w_ref, *refs):
        x_refs, refs = refs[:PER], refs[PER:]
        if last:
            (base_ref, grad_ref), refs = refs[:2], refs[2:]
            out_h, out_a, w_buf, x_buf, total, h_buf, a_buf, grad_buf, sems = refs
        else:
            out, w_buf, x_buf, total, sems = refs
        for j in range(N):
            start(w_ref.at[at_ref[0] ^ j, pl.ds(offset, 2 * width)], w_buf.at[j], sems.at[j])
            place(grouped(x_refs)[j], x_buf.at[j], sems.at[N + j])
        if last:
            first = start(base_ref, total, sems.at[2 * N])
            second = start(grad_ref, grad_buf, sems.at[2 * N + 1])
            first.wait()
        else:
            total[...] = jnp.zeros_like(total)

        def step(j, carry):
            pltpu.make_async_copy(w_ref.at[0, pl.ds(offset, 2 * width)], w_buf.at[j], sems.at[j]).wait()
            pltpu.make_async_copy(x_refs[0], x_buf.at[j], sems.at[N + j]).wait()
            total[...] += dot(x_buf[j, 0], w_buf[j, :width], NN) + dot(x_buf[j, 1], w_buf[j, width:], NN)
            return carry

        lax.fori_loop(0, N, step, 0)
        if last:
            second.wait()
            grad = sum(grad_buf[j].astype(F32) for j in range(N))
            gate, up = total[:, :units], total[:, units:]
            sig = jax.nn.sigmoid(gate)
            h_buf[...] = (gate * sig * up).astype(BF16)
            a_buf[:, :units] = (grad * up * sig * (1.0 + gate * (1.0 - sig))).astype(BF16)
            a_buf[:, units:] = (grad * gate * sig).astype(BF16)
            stores = [start(h_buf, out_h, sems.at[0]), start(a_buf, out_a, sems.at[1])]
        else:
            stores = [start(total, out, sems.at[0])]
        for copy in stores:
            copy.wait()

    scratch = [vmem(N, 2 * width, cols), vmem(N, 2, rows, width), vmem(rows, cols, dtype=F32)]
    if not last:
        return call(body, jax.ShapeDtypeStruct((rows, cols), F32), scratch, [at, w_in] + parts, 2 * N)
    outs = (jax.ShapeDtypeStruct((rows, units), BF16), jax.ShapeDtypeStruct((rows, cols), BF16))
    scratch += [vmem(rows, units), vmem(rows, cols), vmem(N, rows, units)]
    return call(body, outs, scratch, [at, w_in] + parts + [base, grads], 2 * N + 2)


def fetch(chunks, x_refs, x_bufs, sems, base):
    for j in range(N):
        for h in range(len(chunks)):
            place(grouped(x_refs[h * PER :])[j], x_bufs[h].at[j], sems.at[base + h * N + j])


def arrived(x_refs, x_bufs, sems, base, h, j):
    pltpu.make_async_copy(x_refs[h * PER], x_bufs[h].at[j], sems.at[base + h * N + j]).wait()


def flat(chunks):
    return [x for parts in chunks for x in parts]


def buffers(chunks):
    return [vmem(N, *parts[0].shape) for parts in chunks]


def hidden_grads(chunks, w_down, at):
    rows = chunks[0][0].shape[1]
    units, width = w_down.shape
    count = len(chunks)

    def body(at_ref, w_ref, *refs):
        x_refs, (out, w_buf, *x_bufs, out_buf, sems) = refs[: count * PER], refs[count * PER :]
        first = start(w_ref, w_buf, sems.at[0])
        fetch(chunks, x_refs, x_bufs, sems, 1 + N)
        first.wait()

        def step(j, carry):
            total, lo = None, 0
            for h in range(count):
                w = x_bufs[h].shape[3]
                arrived(x_refs, x_bufs, sems, 1 + N, h, j)
                for c in range(2):
                    term = dot(x_bufs[h][j, c], w_buf[:, lo : lo + w], NT)
                    total = term if total is None else total + term
                    lo += w
            out_buf[j] = total.astype(BF16)
            start(out_buf.at[j], out.at[at_ref[0] ^ j], sems.at[1 + j])
            return carry

        lax.fori_loop(0, N, step, 0)
        for j in range(N):
            pltpu.make_async_copy(out_buf.at[j], out.at[0], sems.at[1 + j]).wait()

    scratch = [vmem(units, width)] + buffers(chunks) + [vmem(N, rows, units)]
    out = jax.ShapeDtypeStruct((N, rows, units), BF16)
    return call(body, out, scratch, [at, w_down] + flat(chunks), 1 + N + count * N)


def weight_grad(chunks, acts, at, lo_col):
    rows, cols = acts.shape
    units = cols // 2
    width = sum(2 * parts[0].shape[2] for parts in chunks)
    count = len(chunks)

    def body(at_ref, a_ref, *refs):
        x_refs, (out, a_buf, *x_bufs, out_buf, sems) = refs[: count * PER], refs[count * PER :]
        first = start(a_ref, a_buf, sems.at[0])
        fetch(chunks, x_refs, x_bufs, sems, 1 + N)
        first.wait()

        def step(j, carry):
            lo = 0
            for h in range(count):
                w = x_bufs[h].shape[3]
                arrived(x_refs, x_bufs, sems, 1 + N, h, j)
                for c in range(2):
                    grads = dot(x_bufs[h][j, c], a_buf[:, lo_col : lo_col + units], TN)
                    out_buf[j, lo : lo + w] = grads.astype(BF16)
                    lo += w
            start(out_buf.at[j], out.at[at_ref[0] ^ j], sems.at[1 + j])
            return carry

        lax.fori_loop(0, N, step, 0)
        for j in range(N):
            pltpu.make_async_copy(out_buf.at[j], out.at[0], sems.at[1 + j]).wait()

    scratch = [vmem(rows, cols)] + buffers(chunks) + [vmem(N, width, units)]
    out = jax.ShapeDtypeStruct((N, width, units), BF16)
    return call(body, out, scratch, [at, acts] + flat(chunks), 1 + N + count * N)


def down_grad(chunks, hidden, at):
    _, rows, units = hidden.shape
    width = sum(2 * parts[0].shape[2] for parts in chunks)
    count = len(chunks)

    def body(at_ref, h_ref, *refs):
        x_refs, (out, h_buf, *x_bufs, out_buf, sems) = refs[: count * PER], refs[count * PER :]
        first = start(h_ref, h_buf, sems.at[0])
        fetch(chunks, x_refs, x_bufs, sems, 1)
        out_buf[...] = jnp.zeros_like(out_buf)
        first.wait()

        def step(j, carry):
            lo = 0
            for h in range(count):
                w = x_bufs[h].shape[3]
                arrived(x_refs, x_bufs, sems, 1, h, j)
                for c in range(2):
                    out_buf[:, lo : lo + w] += dot(h_buf[at_ref[0] ^ j], x_bufs[h][j, c], TN)
                    lo += w
            return carry

        lax.fori_loop(0, N, step, 0)
        start(out_buf, out, sems.at[0]).wait()

    scratch = [vmem(N, rows, units)] + buffers(chunks) + [vmem(units, width, dtype=F32)]
    out = jax.ShapeDtypeStruct((units, width), F32)
    return call(body, out, scratch, [at, hidden] + flat(chunks), 1 + count * N)


def input_partials(acts, w_in, at, offset, width):
    rows, cols = acts.shape

    def body(at_ref, a_ref, w_ref, *refs):
        outs, (a_buf, w_buf, out_buf, sems) = refs[: N - 1], refs[N - 1 :]
        first = start(a_ref, a_buf, sems.at[0])
        for j in range(1, N):
            start(w_ref.at[at_ref[0] ^ j, pl.ds(offset, 2 * width)], w_buf.at[j - 1], sems.at[j])
        first.wait()

        def step(j, carry):
            pltpu.make_async_copy(w_ref.at[0, pl.ds(offset, 2 * width)], w_buf.at[j], sems.at[1 + j]).wait()
            for c in range(2):
                out_buf[j, c] = dot(a_buf[...], w_buf[j, c * width : (c + 1) * width], NT).astype(BF16)
            return carry

        lax.fori_loop(0, N - 1, step, 0)
        stores = [start(out_buf.at[j], outs[j], sems.at[j]) for j in range(N - 1)]
        for copy in stores:
            copy.wait()

    outs = (jax.ShapeDtypeStruct((2, rows, width), BF16),) * (N - 1)
    scratch = [vmem(rows, cols), vmem(N - 1, 2 * width, cols), vmem(N - 1, 2, rows, width)]
    return call(body, outs, scratch, [at, acts, w_in], N)


def input_totals(acts, w_in, at, offset, received, order):
    rows, cols = acts.shape
    _, _, width = received[0].shape

    def body(at_ref, a_ref, w_ref, order_ref, *refs):
        r_refs, (out, a_buf, w_buf, o_buf, r_buf, t_buf, out_buf, sems) = refs[: N - 1], refs[N - 1 :]
        copies = [
            start(a_ref, a_buf, sems.at[0]),
            start(w_ref.at[at_ref[0], pl.ds(offset, 2 * width)], w_buf, sems.at[1]),
            start(order_ref, o_buf, sems.at[2]),
        ]
        copies += [start(r_refs[j], r_buf.at[j], sems.at[3 + j]) for j in range(N - 1)]
        for copy in copies:
            copy.wait()
        for c in range(2):
            total = dot(a_buf[...], w_buf[c * width : (c + 1) * width], NT)
            for j in range(N - 1):
                total = total + r_buf[j, c].astype(F32)
            t_buf[c * rows : (c + 1) * rows] = total.astype(BF16)

        def step(i, carry):
            block = pl.ds(i * (rows // 2), rows // 2)
            out_buf[block] = dot(o_buf[block], t_buf[...], NN).astype(BF16)
            return carry

        lax.fori_loop(0, 4, step, 0)
        start(out_buf, out, sems.at[0]).wait()

    scratch = [vmem(rows, cols), vmem(2 * width, cols), vmem(2 * rows, 2 * rows), vmem(N - 1, 2, rows, width)]
    scratch += [vmem(2 * rows, width), vmem(2 * rows, width)]
    out = jax.ShapeDtypeStruct((2 * rows, width), BF16)
    return call(body, out, scratch, [at, acts, w_in, order] + list(received), 3 + N - 1)


def slots_of(route, experts, stride):
    rows, top = route.shape
    expert_of = route.reshape(rows * top)
    onehot = (expert_of[:, None] == jnp.arange(experts, dtype=jnp.int32)[None, :]).astype(jnp.int32)
    earlier = jnp.cumsum(onehot, axis=0) - onehot
    position = jnp.sum(earlier * onehot, axis=1)
    return (expert_of * stride + position).reshape(rows, top)


def per_device(tokens, grad_out, route_ids, combine, gate_weight, up_weight, down_weight):
    rows, width = tokens.shape
    top = route_ids.shape[1]
    groups = lax.axis_size("expert")
    experts = gate_weight.shape[0] * groups
    capacity = min(rows, (5 * top * rows + 4 * experts - 1) // (4 * experts))
    slots = experts * capacity
    piece = (width // 4 + 127) // 128 * 128
    small = width // 2 - piece
    pieces, starts = (small, piece), (0, 2 * small)
    z_pieces, z_starts = (piece, small), (0, 2 * piece)
    at = lax.axis_index("ffn").astype(jnp.int32)[None]

    def swap(x, by):
        return lax.ppermute(x, "ffn", [(i, i ^ by) for i in range(N)])

    def flip(x):
        return lax.ppermute(
            x, ("dp", "ffn"), [(a * N + b, b * N + a) for a in range(N) for b in range(N)]
        )

    def exchange(x):
        return lax.all_to_all(x, "expert", split_axis=0, concat_axis=0, tiled=True)

    def gather_rows(packed):
        received = exchange(packed)
        own = dot(order, received.reshape(2 * slots, -1), NN).astype(BF16).reshape(2, slots, -1)
        near, other = swap(own, 1), swap(own, 3)
        return [own, near, swap(near[0], 3), swap(other[1], 1), other]

    z_local = flip(grad_out)

    to = jnp.arange(2 * slots, dtype=jnp.int32)
    to = to % slots // capacity * (2 * capacity) + to // slots * capacity + to % capacity
    order = (to[:, None] == jnp.arange(2 * slots, dtype=jnp.int32)[None, :]).astype(BF16)
    order_back = (jnp.arange(2 * slots, dtype=jnp.int32)[:, None] == to[None, :]).astype(BF16)

    w_in = jnp.concatenate([gate_weight[0], up_weight[0]], axis=1)
    w_in = lax.all_gather(w_in, "dp", axis=0, tiled=False)

    slot_index = jnp.arange(2 * slots, dtype=jnp.int32)[:, None]

    def hits_of(slot):
        return [[slot_index == (slot[:, k] + c * capacity)[None, :] for k in range(top)] for c in range(2)]

    def one_hot(hits):
        return jnp.concatenate([sum(h.astype(BF16) for h in hit) for hit in hits], axis=1)

    slot = slots_of(route_ids, experts, 2 * capacity)
    x_place = one_hot(hits_of(slot))
    routing = flip(jnp.concatenate([slot.astype(F32), combine], axis=1))
    z_hits = hits_of(routing[:, :top].astype(jnp.int32))
    z_place = one_hot(z_hits)
    z_scale = jnp.zeros((), F32)
    for hit in z_hits:
        for k in range(top):
            z_scale = jnp.where(hit[k], routing[:, top + k][None, :], z_scale)
    z_scale = jnp.sum(z_scale, axis=1)[:, None]

    def stacked(x, lo, w):
        return jnp.concatenate([x[:, lo : lo + w], x[:, lo + w : lo + 2 * w]], axis=0)

    def pack_x(h):
        return dot(x_place, stacked(tokens, starts[h], pieces[h]), NN).astype(BF16).reshape(groups, 2 * capacity, -1)

    def pack_z(h):
        packed = dot(z_place, stacked(z_local, z_starts[h], z_pieces[h]), NN) * z_scale
        return packed.astype(BF16).reshape(groups, 2 * capacity, -1)

    x_0 = gather_rows(pack_x(0))
    z_0 = gather_rows(pack_z(0))
    z_1 = gather_rows(pack_z(1))
    x_1 = gather_rows(pack_x(1))

    partial = hidden_grads((z_0, z_1), down_weight[0], at)
    grads = lax.all_to_all(partial, "dp", split_axis=0, concat_axis=0, tiled=True)
    base = project(x_0, w_in, at, starts[0])
    hidden, acts = project(x_1, w_in, at, starts[1], base, grads)

    part_gate = weight_grad((x_0, x_1), acts, at, 0)
    grad_gate = lax.psum_scatter(part_gate, "dp", scatter_dimension=0, tiled=True)
    grad_gate = grad_gate.astype(F32)
    leads = []
    for h in range(2):
        leads.append(input_partials(acts, w_in, at, starts[h], pieces[h]))
    received = []
    for h in range(2):
        received.append([swap(leads[h][j - 1], j) for j in range(1, N)])
    part_up = weight_grad((x_0, x_1), acts, at, gate_weight.shape[2])
    grad_up = lax.psum_scatter(part_up, "dp", scatter_dimension=0, tiled=True).astype(F32)

    grad_tokens = []
    hidden_all = lax.all_gather(hidden, "dp", axis=0, tiled=False)
    received[1], hidden_all, grad_gate = lax.optimization_barrier((received[1], hidden_all, grad_gate))
    for h in range(2):
        total = input_totals(acts, w_in, at, starts[h], received[h], order_back)
        back = exchange(total.reshape(groups, 2 * capacity, -1))
        back = back.reshape(2 * slots, -1)
        back = dot(x_place, back, TN).astype(BF16)
        grad_tokens += [back[:rows], back[rows:]]
    grad_tokens = jnp.concatenate(grad_tokens, axis=1)

    grad_down = down_grad((z_0, z_1), hidden_all, at)[None]
    return grad_tokens, grad_gate, grad_up, grad_down


def solution(mesh):
    return jax.shard_map(
        per_device,
        mesh=mesh,
        in_specs=(
            P(("dp", "expert"), "ffn"),
            P(("dp", "expert"), "ffn"),
            P(("dp", "expert"), None),
            P(("dp", "expert"), None),
            P("expert", "dp", "ffn"),
            P("expert", "dp", "ffn"),
            P("expert", "ffn", "dp"),
        ),
        out_specs=(
            P(("dp", "expert"), "ffn"),
            P("expert", "dp", "ffn"),
            P("expert", "dp", "ffn"),
            P("expert", "ffn", "dp"),
        ),
        check_vma=False,
    )
```

```python
import jax
import jax.numpy as jnp
from jax import lax
from jax.experimental import pallas as pl
from jax.experimental.pallas import tpu as pltpu
from jax.sharding import PartitionSpec as P


F32 = jnp.float32
BF16 = jnp.bfloat16
N = 4
ANY = pl.BlockSpec(memory_space=pl.ANY)
SMEM = pl.BlockSpec(memory_space=pltpu.SMEM)


def dot(a, b, contract):
    return lax.dot_general(a, b, (contract, ((), ())), preferred_element_type=F32)


NN, NT, TN = ((1,), (0,)), ((1,), (1,)), ((0,), (0,))


def call(body, outs, scratch, args, copies):
    return pl.pallas_call(
        body,
        out_shape=outs,
        in_specs=[SMEM] + [ANY] * (len(args) - 1),
        out_specs=jax.tree.map(lambda _: ANY, outs),
        scratch_shapes=list(scratch) + [pltpu.SemaphoreType.DMA((copies,))],
    )(*args)


def start(src, dst, sem):
    copy = pltpu.make_async_copy(src, dst, sem)
    copy.start()
    return copy


def place(part, buf, sem):
    if len(part) == 1:
        start(part[0], buf, sem)
    else:
        for c in range(2):
            start(part[c], buf.at[c], sem)


def grouped(refs):
    return [[refs[0]], [refs[1]], [refs[2], refs[3]], [refs[4]]]


PER = N + 1


def vmem(*shape, dtype=BF16):
    return pltpu.VMEM(shape, dtype)


def project(groups, w_in, at, base=None, grads=None):
    rows = groups[0][2][0].shape[1]
    cols = w_in.shape[2]
    units = cols // 2
    last = base is not None
    arrays = [x for _, js, parts in groups for j in js for x in grouped(parts)[j]]
    widths = [parts[0].shape[2] for _, _, parts in groups]
    count = sum(len(js) for _, js, _ in groups)

    def body(at_ref, w_ref, *refs):
        x_refs, refs = refs[: len(arrays)], refs[len(arrays) :]
        if last:
            (base_ref, grad_ref, out_h, out_a), refs = refs[:4], refs[4:]
        else:
            (out,), refs = refs[:1], refs[1:]
        w_bufs, x_bufs, refs = refs[: len(groups)], refs[len(groups) : 2 * len(groups)], refs[2 * len(groups) :]
        total, sems = refs[0], refs[-1]
        array, sem = 0, 0
        for g, (offset, js, parts) in enumerate(groups):
            for i, j in enumerate(js):
                size = len(grouped(parts)[j])
                start(w_ref.at[at_ref[0] ^ j, pl.ds(offset, 2 * widths[g])], w_bufs[g].at[i], sems.at[sem])
                place(x_refs[array : array + size], x_bufs[g].at[i], sems.at[count + sem])
                array, sem = array + size, sem + 1
        if last:
            h_buf, a_buf, grad_buf = refs[1:4]
            first = start(base_ref, total, sems.at[2 * count])
            second = start(grad_ref, grad_buf, sems.at[2 * count + 1])
            first.wait()
        else:
            total[...] = jnp.zeros_like(total)
        sem = 0
        for g, (offset, js, _) in enumerate(groups):
            width, w_buf, x_buf, lo = widths[g], w_bufs[g], x_bufs[g], sem

            def step(i, carry, width=width, w_buf=w_buf, x_buf=x_buf, lo=lo, offset=offset):
                pltpu.make_async_copy(w_ref.at[0, pl.ds(offset, 2 * width)], w_buf.at[i], sems.at[lo + i]).wait()
                pltpu.make_async_copy(x_buf.at[i], x_buf.at[i], sems.at[count + lo + i]).wait()
                total[...] += dot(x_buf[i, 0], w_buf[i, :width], NN) + dot(x_buf[i, 1], w_buf[i, width:], NN)
                return carry

            lax.fori_loop(0, len(js), step, 0)
            sem += len(js)
        if last:
            second.wait()
            grad = sum(grad_buf[j].astype(F32) for j in range(N))
            gate, up = total[:, :units], total[:, units:]
            sig = jax.nn.sigmoid(gate)
            h_buf[...] = (gate * sig * up).astype(BF16)
            a_buf[:, :units] = (grad * up * sig * (1.0 + gate * (1.0 - sig))).astype(BF16)
            a_buf[:, units:] = (grad * gate * sig).astype(BF16)
            stores = [start(h_buf, out_h, sems.at[0]), start(a_buf, out_a, sems.at[1])]
        else:
            stores = [start(total, out, sems.at[0])]
        for copy in stores:
            copy.wait()

    scratch = [vmem(len(js), 2 * w, cols) for (_, js, _), w in zip(groups, widths)]
    scratch += [vmem(len(js), 2, rows, w) for (_, js, _), w in zip(groups, widths)] + [vmem(rows, cols, dtype=F32)]
    if not last:
        return call(body, jax.ShapeDtypeStruct((rows, cols), F32), scratch, [at, w_in] + arrays, 2 * count)
    outs = (jax.ShapeDtypeStruct((rows, units), BF16), jax.ShapeDtypeStruct((rows, cols), BF16))
    scratch += [vmem(rows, units), vmem(rows, cols), vmem(N, rows, units)]
    return call(body, outs, scratch, [at, w_in] + arrays + [base, grads], 2 * count + 2)


def fetch(chunks, x_refs, x_bufs, sems, base):
    for j in range(N):
        for h in range(len(chunks)):
            place(grouped(x_refs[h * PER :])[j], x_bufs[h].at[j], sems.at[base + h * N + j])


def arrived(x_refs, x_bufs, sems, base, h, j):
    pltpu.make_async_copy(x_refs[h * PER], x_bufs[h].at[j], sems.at[base + h * N + j]).wait()


def flat(chunks):
    return [x for parts in chunks for x in parts]


def buffers(chunks):
    return [vmem(N, *parts[0].shape) for parts in chunks]


def hidden_grads(chunks, w_down, at):
    rows = chunks[0][0].shape[1]
    units, width = w_down.shape
    count = len(chunks)

    def body(at_ref, w_ref, *refs):
        x_refs, (out, w_buf, *x_bufs, out_buf, sems) = refs[: count * PER], refs[count * PER :]
        first = start(w_ref, w_buf, sems.at[0])
        fetch(chunks, x_refs, x_bufs, sems, 1 + N)
        first.wait()

        def step(j, carry):
            total, lo = None, 0
            for h in range(count):
                w = x_bufs[h].shape[3]
                arrived(x_refs, x_bufs, sems, 1 + N, h, j)
                for c in range(2):
                    term = dot(x_bufs[h][j, c], w_buf[:, lo : lo + w], NT)
                    total = term if total is None else total + term
                    lo += w
            out_buf[j] = total.astype(BF16)
            start(out_buf.at[j], out.at[at_ref[0] ^ j], sems.at[1 + j])
            return carry

        lax.fori_loop(0, N, step, 0)
        for j in range(N):
            pltpu.make_async_copy(out_buf.at[j], out.at[0], sems.at[1 + j]).wait()

    scratch = [vmem(units, width)] + buffers(chunks) + [vmem(N, rows, units)]
    out = jax.ShapeDtypeStruct((N, rows, units), BF16)
    return call(body, out, scratch, [at, w_down] + flat(chunks), 1 + N + count * N)


def weight_grad(chunks, acts, at, lo_col, relative=False):
    rows, cols = acts.shape
    units = cols // 2
    width = sum(2 * parts[0].shape[2] for parts in chunks)
    count = len(chunks)

    def body(at_ref, a_ref, *refs):
        x_refs, (out, a_buf, *x_bufs, out_buf, sems) = refs[: count * PER], refs[count * PER :]
        first = start(a_ref, a_buf, sems.at[0])
        fetch(chunks, x_refs, x_bufs, sems, 1 + N)
        first.wait()

        def step(j, carry):
            lo = 0
            for h in range(count):
                w = x_bufs[h].shape[3]
                arrived(x_refs, x_bufs, sems, 1 + N, h, j)

                def piece(c, carry, h=h, lo=lo, w=w):
                    grads = dot(x_bufs[h][j, c], a_buf[:, lo_col : lo_col + units], TN)
                    out_buf[j, pl.ds(pl.multiple_of(lo + c * w, 128), w)] = grads.astype(BF16)
                    return carry

                lax.fori_loop(0, 2, piece, 0)
                lo += 2 * w
            to = at_ref[0] ^ j ^ at_ref[1] if relative else at_ref[0] ^ j
            start(out_buf.at[j], out.at[to], sems.at[1 + j])
            return carry

        lax.fori_loop(0, N, step, 0)
        for j in range(N):
            pltpu.make_async_copy(out_buf.at[j], out.at[0], sems.at[1 + j]).wait()

    scratch = [vmem(rows, cols)] + buffers(chunks) + [vmem(N, width, units)]
    out = jax.ShapeDtypeStruct((N, width, units), BF16)
    return call(body, out, scratch, [at, acts] + flat(chunks), 1 + N + count * N)


def down_grad(chunks, hidden, at):
    _, rows, units = hidden.shape
    width = sum(2 * parts[0].shape[2] for parts in chunks)
    count = len(chunks)

    def body(at_ref, h_ref, *refs):
        x_refs, (out, h_buf, *x_bufs, out_buf, sems) = refs[: count * PER], refs[count * PER :]
        first = start(h_ref, h_buf, sems.at[0])
        fetch(chunks, x_refs, x_bufs, sems, 1)
        out_buf[...] = jnp.zeros_like(out_buf)
        first.wait()

        def step(j, carry):
            lo = 0
            for h in range(count):
                w = x_bufs[h].shape[3]
                arrived(x_refs, x_bufs, sems, 1, h, j)

                def piece(c, carry, h=h, lo=lo, w=w):
                    out_buf[:, pl.ds(pl.multiple_of(lo + c * w, 128), w)] += dot(
                        h_buf[at_ref[0] ^ j], x_bufs[h][j, c], TN
                    )
                    return carry

                lax.fori_loop(0, 2, piece, 0)
                lo += 2 * w
            return carry

        lax.fori_loop(0, N, step, 0)
        start(out_buf, out, sems.at[0]).wait()

    scratch = [vmem(N, rows, units)] + buffers(chunks) + [vmem(units, width, dtype=F32)]
    out = jax.ShapeDtypeStruct((units, width), F32)
    return call(body, out, scratch, [at, hidden] + flat(chunks), 1 + count * N)


def input_partials(acts, w_in, at, offset, width):
    rows, cols = acts.shape

    def body(at_ref, a_ref, w_ref, *refs):
        outs, (a_buf, w_buf, out_buf, sems) = refs[: N - 1], refs[N - 1 :]
        first = start(a_ref, a_buf, sems.at[0])
        for j in range(1, N):
            start(w_ref.at[at_ref[0] ^ j, pl.ds(offset, 2 * width)], w_buf.at[j - 1], sems.at[j])
        first.wait()

        def step(j, carry):
            pltpu.make_async_copy(w_ref.at[0, pl.ds(offset, 2 * width)], w_buf.at[j], sems.at[1 + j]).wait()

            def piece(c, carry):
                w = w_buf[j, pl.ds(pl.multiple_of(c * width, 128), width)]
                out_buf[j, c] = dot(a_buf[...], w, NT).astype(BF16)
                return carry

            return lax.fori_loop(0, 2, piece, carry)

        lax.fori_loop(0, N - 1, step, 0)
        stores = [start(out_buf.at[j], outs[j], sems.at[j]) for j in range(N - 1)]
        for copy in stores:
            copy.wait()

    outs = (jax.ShapeDtypeStruct((2, rows, width), BF16),) * (N - 1)
    scratch = [vmem(rows, cols), vmem(N - 1, 2 * width, cols), vmem(N - 1, 2, rows, width)]
    return call(body, outs, scratch, [at, acts, w_in], N)


def input_totals(acts, w_in, at, offset, received, order):
    rows, cols = acts.shape
    _, _, width = received[0].shape

    def body(at_ref, a_ref, w_ref, order_ref, *refs):
        r_refs, (out, a_buf, w_buf, o_buf, r_buf, t_buf, out_buf, sems) = refs[: N - 1], refs[N - 1 :]
        copies = [
            start(a_ref, a_buf, sems.at[0]),
            start(w_ref.at[at_ref[0], pl.ds(offset, 2 * width)], w_buf, sems.at[1]),
            start(order_ref, o_buf, sems.at[2]),
        ]
        copies += [start(r_refs[j], r_buf.at[j], sems.at[3 + j]) for j in range(N - 1)]
        for copy in copies:
            copy.wait()

        def piece(c, carry):
            total = dot(a_buf[...], w_buf[pl.ds(pl.multiple_of(c * width, 128), width)], NT)
            for j in range(N - 1):
                total = total + r_buf[j, c].astype(F32)
            t_buf[pl.ds(pl.multiple_of(c * rows, rows), rows)] = total.astype(BF16)
            return carry

        lax.fori_loop(0, 2, piece, 0)

        def step(i, carry):
            block = pl.ds(i * (rows // 2), rows // 2)
            out_buf[block] = dot(o_buf[block], t_buf[...], NN).astype(BF16)
            return carry

        lax.fori_loop(0, 4, step, 0)
        start(out_buf, out, sems.at[0]).wait()

    scratch = [vmem(rows, cols), vmem(2 * width, cols), vmem(2 * rows, 2 * rows), vmem(N - 1, 2, rows, width)]
    scratch += [vmem(2 * rows, width), vmem(2 * rows, width)]
    out = jax.ShapeDtypeStruct((2 * rows, width), BF16)
    return call(body, out, scratch, [at, acts, w_in, order] + list(received), 3 + N - 1)


def slots_of(route, experts, stride):
    rows, top = route.shape
    expert_of = route.reshape(rows * top)
    onehot = (expert_of[:, None] == jnp.arange(experts, dtype=jnp.int32)[None, :]).astype(jnp.int32)
    earlier = jnp.cumsum(onehot, axis=0) - onehot
    position = jnp.sum(earlier * onehot, axis=1)
    return (expert_of * stride + position).reshape(rows, top)


def per_device(tokens, grad_out, route_ids, combine, gate_weight, up_weight, down_weight):
    rows, width = tokens.shape
    top = route_ids.shape[1]
    groups = lax.axis_size("expert")
    experts = gate_weight.shape[0] * groups
    capacity = min(rows, (5 * top * rows + 4 * experts - 1) // (4 * experts))
    slots = experts * capacity
    piece = (width // 4 + 127) // 128 * 128
    small = width // 2 - piece
    pieces, starts = (small, piece), (0, 2 * small)
    z_pieces, z_starts = (piece, small), (0, 2 * piece)
    at = jnp.stack([lax.axis_index("ffn"), lax.axis_index("dp")]).astype(jnp.int32)

    def swap(x, by, axis="ffn"):
        return lax.ppermute(x, axis, [(i, i ^ by) for i in range(N)])

    def flip(x):
        return lax.ppermute(
            x, ("dp", "ffn"), [(a * N + b, b * N + a) for a in range(N) for b in range(N)]
        )

    def exchange(x):
        return lax.all_to_all(x, "expert", split_axis=0, concat_axis=0, tiled=True)

    def gather_rows(packed):
        received = exchange(packed)
        own = dot(order, received.reshape(2 * slots, -1), NN).astype(BF16).reshape(2, slots, -1)
        near, other = swap(own, 1), swap(own, 3)
        return [own, near, swap(near[0], 3), swap(other[1], 1), other]

    z_local = flip(grad_out)

    to = jnp.arange(2 * slots, dtype=jnp.int32)
    to = to % slots // capacity * (2 * capacity) + to // slots * capacity + to % capacity
    order = (to[:, None] == jnp.arange(2 * slots, dtype=jnp.int32)[None, :]).astype(BF16)
    order_back = (jnp.arange(2 * slots, dtype=jnp.int32)[:, None] == to[None, :]).astype(BF16)

    w_in = jnp.concatenate([gate_weight[0], up_weight[0]], axis=1)
    w_in = lax.all_gather(w_in, "dp", axis=0, tiled=False)

    slot_index = jnp.arange(2 * slots, dtype=jnp.int32)[:, None]

    def hits_of(slot):
        return [[slot_index == (slot[:, k] + c * capacity)[None, :] for k in range(top)] for c in range(2)]

    def one_hot(hits):
        return jnp.concatenate([sum(h.astype(BF16) for h in hit) for hit in hits], axis=1)

    slot = slots_of(route_ids, experts, 2 * capacity)
    x_place = one_hot(hits_of(slot))
    routing = flip(jnp.concatenate([slot.astype(F32), combine], axis=1))
    z_hits = hits_of(routing[:, :top].astype(jnp.int32))
    z_place = one_hot(z_hits)
    z_scale = jnp.zeros((), F32)
    for hit in z_hits:
        for k in range(top):
            z_scale = jnp.where(hit[k], routing[:, top + k][None, :], z_scale)
    z_scale = jnp.sum(z_scale, axis=1)[:, None]

    def stacked(x, lo, w):
        return jnp.concatenate([x[:, lo : lo + w], x[:, lo + w : lo + 2 * w]], axis=0)

    def pack_x(h):
        return dot(x_place, stacked(tokens, starts[h], pieces[h]), NN).astype(BF16).reshape(groups, 2 * capacity, -1)

    def pack_z(h):
        packed = dot(z_place, stacked(z_local, z_starts[h], z_pieces[h]), NN) * z_scale
        return packed.astype(BF16).reshape(groups, 2 * capacity, -1)

    x_0 = gather_rows(pack_x(0))
    z_0 = gather_rows(pack_z(0))
    z_1 = gather_rows(pack_z(1))
    x_1 = gather_rows(pack_x(1))

    partial = hidden_grads((z_0, z_1), down_weight[0], at)
    grads = lax.all_to_all(partial, "dp", split_axis=0, concat_axis=0, tiled=True)
    base = project([(starts[0], (0, 1, 2, 3), x_0), (starts[1], (0, 1, 3), x_1)], w_in, at)
    hidden, acts = project([(starts[1], (2,), x_1)], w_in, at, base, grads)

    part_gate = weight_grad((x_0, x_1), acts, at, 0)
    grad_gate = lax.psum_scatter(part_gate, "dp", scatter_dimension=0, tiled=True)
    grad_gate = grad_gate.astype(F32)
    leads = []
    for h in range(2):
        leads.append(input_partials(acts, w_in, at, starts[h], pieces[h]))
    received = []
    for h in range(2):
        received.append([swap(leads[h][j - 1], j) for j in range(1, N)])
    direct = weight_grad((x_0,), acts, at, gate_weight.shape[2], relative=True)
    scattered = weight_grad((x_1,), acts, at, gate_weight.shape[2])
    scattered = lax.psum_scatter(scattered, "dp", scatter_dimension=0, tiled=True)
    direct = [direct[0]] + [swap(direct[j], j, "dp") for j in range(1, N)]
    direct = sum(d.astype(F32) for d in direct)
    grad_up = jnp.concatenate([direct[None], scattered.astype(F32)], axis=1)

    grad_tokens = []
    hidden_all = lax.all_gather(hidden, "dp", axis=0, tiled=False)
    received[1], hidden_all, grad_gate = lax.optimization_barrier((received[1], hidden_all, grad_gate))
    for h in range(2):
        total = input_totals(acts, w_in, at, starts[h], received[h], order_back)
        back = exchange(total.reshape(groups, 2 * capacity, -1))
        back = back.reshape(2 * slots, -1)
        back = dot(x_place, back, TN).astype(BF16)
        grad_tokens += [back[:rows], back[rows:]]
    grad_tokens = jnp.concatenate(grad_tokens, axis=1)

    grad_down = down_grad((z_0, z_1), hidden_all, at)[None]
    return grad_tokens, grad_gate, grad_up, grad_down


def solution(mesh):
    return jax.shard_map(
        per_device,
        mesh=mesh,
        in_specs=(
            P(("dp", "expert"), "ffn"),
            P(("dp", "expert"), "ffn"),
            P(("dp", "expert"), None),
            P(("dp", "expert"), None),
            P("expert", "dp", "ffn"),
            P("expert", "dp", "ffn"),
            P("expert", "ffn", "dp"),
        ),
        out_specs=(
            P(("dp", "expert"), "ffn"),
            P("expert", "dp", "ffn"),
            P("expert", "dp", "ffn"),
            P("expert", "ffn", "dp"),
        ),
        check_vma=False,
    )
```

```python
import jax
import jax.numpy as jnp
from jax import lax
from jax.experimental import pallas as pl
from jax.experimental.pallas import tpu as pltpu
from jax.sharding import PartitionSpec as P


F32 = jnp.float32
BF16 = jnp.bfloat16
N = 4
ANY = pl.BlockSpec(memory_space=pl.ANY)
SMEM = pl.BlockSpec(memory_space=pltpu.SMEM)


def dot(a, b, contract):
    return lax.dot_general(a, b, (contract, ((), ())), preferred_element_type=F32)


NN, NT, TN = ((1,), (0,)), ((1,), (1,)), ((0,), (0,))


def call(body, outs, scratch, args, copies):
    return pl.pallas_call(
        body,
        out_shape=outs,
        in_specs=[SMEM] + [ANY] * (len(args) - 1),
        out_specs=jax.tree.map(lambda _: ANY, outs),
        scratch_shapes=list(scratch) + [pltpu.SemaphoreType.DMA((copies,))],
    )(*args)


def start(src, dst, sem):
    copy = pltpu.make_async_copy(src, dst, sem)
    copy.start()
    return copy


def slice_of(at, size):
    return pl.ds(at if isinstance(at, int) else pl.multiple_of(at, 128), size)


def place(part, buf, sem):
    if len(part) == 1:
        start(part[0], buf, sem)
    else:
        for c in range(2):
            start(part[c], buf.at[c], sem)


def grouped(refs):
    return [[refs[0]], [refs[1]], [refs[2], refs[3]], [refs[4]]]


PER = N + 1


def vmem(*shape, dtype=BF16):
    return pltpu.VMEM(shape, dtype)


def project(groups, w_in, at, base=None, grads=None):
    rows = groups[0][2][0].shape[1]
    cols = w_in.shape[2]
    units = cols // 2
    last = base is not None
    arrays = [x for _, js, parts in groups for j in js for x in grouped(parts)[j]]
    widths = [parts[0].shape[2] for _, _, parts in groups]
    count = sum(len(js) for _, js, _ in groups)

    def body(at_ref, w_ref, *refs):
        x_refs, refs = refs[: len(arrays)], refs[len(arrays) :]
        if last:
            (base_ref, grad_ref, out_h, out_a), refs = refs[:4], refs[4:]
        else:
            (out,), refs = refs[:1], refs[1:]
        w_bufs, x_bufs, refs = refs[: len(groups)], refs[len(groups) : 2 * len(groups)], refs[2 * len(groups) :]
        total, sems = refs[0], refs[-1]
        array, sem = 0, 0
        for g, (offset, js, parts) in enumerate(groups):
            for i, j in enumerate(js):
                size = len(grouped(parts)[j])
                start(w_ref.at[at_ref[0] ^ j, pl.ds(offset, 2 * widths[g])], w_bufs[g].at[i], sems.at[sem])
                place(x_refs[array : array + size], x_bufs[g].at[i], sems.at[count + sem])
                array, sem = array + size, sem + 1
        if last:
            h_buf, a_buf, grad_buf = refs[1:4]
            first = start(base_ref, total, sems.at[2 * count])
            second = start(grad_ref, grad_buf, sems.at[2 * count + 1])
            first.wait()
        else:
            total[...] = jnp.zeros_like(total)
        sem = 0
        for g, (offset, js, _) in enumerate(groups):
            width, w_buf, x_buf, lo = widths[g], w_bufs[g], x_bufs[g], sem

            def step(i, carry, width=width, w_buf=w_buf, x_buf=x_buf, lo=lo, offset=offset):
                pltpu.make_async_copy(w_ref.at[0, pl.ds(offset, 2 * width)], w_buf.at[i], sems.at[lo + i]).wait()
                pltpu.make_async_copy(x_buf.at[i], x_buf.at[i], sems.at[count + lo + i]).wait()
                total[...] += dot(x_buf[i, 0], w_buf[i, :width], NN) + dot(x_buf[i, 1], w_buf[i, width:], NN)
                return carry

            lax.fori_loop(0, len(js), step, 0)
            sem += len(js)
        if last:
            second.wait()
            grad = sum(grad_buf[j].astype(F32) for j in range(N))
            gate, up = total[:, :units], total[:, units:]
            sig = jax.nn.sigmoid(gate)
            h_buf[...] = (gate * sig * up).astype(BF16)
            a_buf[:, :units] = (grad * up * sig * (1.0 + gate * (1.0 - sig))).astype(BF16)
            a_buf[:, units:] = (grad * gate * sig).astype(BF16)
            stores = [start(h_buf, out_h, sems.at[0]), start(a_buf, out_a, sems.at[1])]
        else:
            stores = [start(total, out, sems.at[0])]
        for copy in stores:
            copy.wait()

    scratch = [vmem(len(js), 2 * w, cols) for (_, js, _), w in zip(groups, widths)]
    scratch += [vmem(len(js), 2, rows, w) for (_, js, _), w in zip(groups, widths)] + [vmem(rows, cols, dtype=F32)]
    if not last:
        return call(body, jax.ShapeDtypeStruct((rows, cols), F32), scratch, [at, w_in] + arrays, 2 * count)
    outs = (jax.ShapeDtypeStruct((rows, units), BF16), jax.ShapeDtypeStruct((rows, cols), BF16))
    scratch += [vmem(rows, units), vmem(rows, cols), vmem(N, rows, units)]
    return call(body, outs, scratch, [at, w_in] + arrays + [base, grads], 2 * count + 2)


def fetch(chunks, x_refs, x_bufs, sems, base):
    for j in range(N):
        for h in range(len(chunks)):
            place(grouped(x_refs[h * PER :])[j], x_bufs[h].at[j], sems.at[base + h * N + j])


def arrived(x_refs, x_bufs, sems, base, h, j):
    pltpu.make_async_copy(x_refs[h * PER], x_bufs[h].at[j], sems.at[base + h * N + j]).wait()


def flat(chunks):
    return [x for parts in chunks for x in parts]


def buffers(chunks):
    return [vmem(N, *parts[0].shape) for parts in chunks]


def hidden_grads(chunks, w_down, at):
    rows = chunks[0][0].shape[1]
    units, width = w_down.shape
    count = len(chunks)

    def body(at_ref, w_ref, *refs):
        x_refs, (out, w_buf, *x_bufs, out_buf, sems) = refs[: count * PER], refs[count * PER :]
        first = start(w_ref, w_buf, sems.at[0])
        fetch(chunks, x_refs, x_bufs, sems, 1 + N)
        first.wait()

        def step(j, carry):
            total, lo = None, 0
            for h in range(count):
                w = x_bufs[h].shape[3]
                arrived(x_refs, x_bufs, sems, 1 + N, h, j)
                for c in range(2):
                    term = dot(x_bufs[h][j, c], w_buf[:, lo : lo + w], NT)
                    total = term if total is None else total + term
                    lo += w
            out_buf[j] = total.astype(BF16)
            start(out_buf.at[j], out.at[at_ref[0] ^ j], sems.at[1 + j])
            return carry

        lax.fori_loop(0, N, step, 0)
        for j in range(N):
            pltpu.make_async_copy(out_buf.at[j], out.at[0], sems.at[1 + j]).wait()

    scratch = [vmem(units, width)] + buffers(chunks) + [vmem(N, rows, units)]
    out = jax.ShapeDtypeStruct((N, rows, units), BF16)
    return call(body, out, scratch, [at, w_down] + flat(chunks), 1 + N + count * N)


def weight_grad(chunks, acts, at, lo_col, relative=False, unroll=False):
    rows, cols = acts.shape
    units = cols // 2
    width = sum(2 * parts[0].shape[2] for parts in chunks)
    count = len(chunks)

    def body(at_ref, a_ref, *refs):
        x_refs, (out, a_buf, *x_bufs, out_buf, sems) = refs[: count * PER], refs[count * PER :]
        first = start(a_ref, a_buf, sems.at[0])
        fetch(chunks, x_refs, x_bufs, sems, 1 + N)
        first.wait()

        def step(j, carry):
            lo = 0
            for h in range(count):
                w = x_bufs[h].shape[3]
                arrived(x_refs, x_bufs, sems, 1 + N, h, j)

                def piece(c, carry, h=h, lo=lo, w=w):
                    grads = dot(x_bufs[h][j, c], a_buf[:, lo_col : lo_col + units], TN)
                    out_buf[j, slice_of(lo + c * w, w)] = grads.astype(BF16)
                    return carry

                if unroll:
                    for c in range(2):
                        piece(c, 0)
                else:
                    lax.fori_loop(0, 2, piece, 0)
                lo += 2 * w
            to = at_ref[0] ^ j ^ at_ref[1] if relative else at_ref[0] ^ j
            start(out_buf.at[j], out.at[to], sems.at[1 + j])
            return carry

        lax.fori_loop(0, N, step, 0)
        for j in range(N):
            pltpu.make_async_copy(out_buf.at[j], out.at[0], sems.at[1 + j]).wait()

    scratch = [vmem(rows, cols)] + buffers(chunks) + [vmem(N, width, units)]
    out = jax.ShapeDtypeStruct((N, width, units), BF16)
    return call(body, out, scratch, [at, acts] + flat(chunks), 1 + N + count * N)


def down_grad(chunks, hidden, at):
    _, rows, units = hidden.shape
    width = sum(2 * parts[0].shape[2] for parts in chunks)
    count = len(chunks)

    def body(at_ref, h_ref, *refs):
        x_refs, (out, h_buf, *x_bufs, out_buf, sems) = refs[: count * PER], refs[count * PER :]
        first = start(h_ref, h_buf, sems.at[0])
        fetch(chunks, x_refs, x_bufs, sems, 1)
        out_buf[...] = jnp.zeros_like(out_buf)
        first.wait()

        def step(j, carry):
            lo = 0
            for h in range(count):
                w = x_bufs[h].shape[3]
                arrived(x_refs, x_bufs, sems, 1, h, j)

                def piece(c, carry, h=h, lo=lo, w=w):
                    out_buf[:, pl.ds(pl.multiple_of(lo + c * w, 128), w)] += dot(
                        h_buf[at_ref[0] ^ j], x_bufs[h][j, c], TN
                    )
                    return carry

                lax.fori_loop(0, 2, piece, 0)
                lo += 2 * w
            return carry

        lax.fori_loop(0, N, step, 0)
        start(out_buf, out, sems.at[0]).wait()

    scratch = [vmem(N, rows, units)] + buffers(chunks) + [vmem(units, width, dtype=F32)]
    out = jax.ShapeDtypeStruct((units, width), F32)
    return call(body, out, scratch, [at, hidden] + flat(chunks), 1 + count * N)


def input_partials(acts, w_in, at, offset, width):
    rows, cols = acts.shape

    def body(at_ref, a_ref, w_ref, *refs):
        outs, (a_buf, w_buf, out_buf, sems) = refs[: N - 1], refs[N - 1 :]
        first = start(a_ref, a_buf, sems.at[0])
        for j in range(1, N):
            start(w_ref.at[at_ref[0] ^ j, pl.ds(offset, 2 * width)], w_buf.at[j - 1], sems.at[j])
        first.wait()

        def step(j, carry):
            pltpu.make_async_copy(w_ref.at[0, pl.ds(offset, 2 * width)], w_buf.at[j], sems.at[1 + j]).wait()

            def piece(c, carry):
                w = w_buf[j, pl.ds(pl.multiple_of(c * width, 128), width)]
                out_buf[j, c] = dot(a_buf[...], w, NT).astype(BF16)
                return carry

            return lax.fori_loop(0, 2, piece, carry)

        lax.fori_loop(0, N - 1, step, 0)
        stores = [start(out_buf.at[j], outs[j], sems.at[j]) for j in range(N - 1)]
        for copy in stores:
            copy.wait()

    outs = (jax.ShapeDtypeStruct((2, rows, width), BF16),) * (N - 1)
    scratch = [vmem(rows, cols), vmem(N - 1, 2 * width, cols), vmem(N - 1, 2, rows, width)]
    return call(body, outs, scratch, [at, acts, w_in], N)


def input_totals(acts, w_in, at, offset, received, order):
    rows, cols = acts.shape
    _, _, width = received[0].shape

    def body(at_ref, a_ref, w_ref, order_ref, *refs):
        r_refs, (out, a_buf, w_buf, o_buf, r_buf, t_buf, out_buf, sems) = refs[: N - 1], refs[N - 1 :]
        copies = [
            start(a_ref, a_buf, sems.at[0]),
            start(w_ref.at[at_ref[0], pl.ds(offset, 2 * width)], w_buf, sems.at[1]),
            start(order_ref, o_buf, sems.at[2]),
        ]
        copies += [start(r_refs[j], r_buf.at[j], sems.at[3 + j]) for j in range(N - 1)]
        for copy in copies:
            copy.wait()

        def piece(c, carry):
            total = dot(a_buf[...], w_buf[pl.ds(pl.multiple_of(c * width, 128), width)], NT)
            for j in range(N - 1):
                total = total + r_buf[j, c].astype(F32)
            t_buf[pl.ds(pl.multiple_of(c * rows, rows), rows)] = total.astype(BF16)
            return carry

        lax.fori_loop(0, 2, piece, 0)

        def step(i, carry):
            block = pl.ds(i * (rows // 2), rows // 2)
            out_buf[block] = dot(o_buf[block], t_buf[...], NN).astype(BF16)
            return carry

        lax.fori_loop(0, 4, step, 0)
        start(out_buf, out, sems.at[0]).wait()

    scratch = [vmem(rows, cols), vmem(2 * width, cols), vmem(2 * rows, 2 * rows), vmem(N - 1, 2, rows, width)]
    scratch += [vmem(2 * rows, width), vmem(2 * rows, width)]
    out = jax.ShapeDtypeStruct((2 * rows, width), BF16)
    return call(body, out, scratch, [at, acts, w_in, order] + list(received), 3 + N - 1)


def slots_of(route, experts, stride):
    rows, top = route.shape
    expert_of = route.reshape(rows * top)
    onehot = (expert_of[:, None] == jnp.arange(experts, dtype=jnp.int32)[None, :]).astype(jnp.int32)
    earlier = jnp.cumsum(onehot, axis=0) - onehot
    position = jnp.sum(earlier * onehot, axis=1)
    return (expert_of * stride + position).reshape(rows, top)


def per_device(tokens, grad_out, route_ids, combine, gate_weight, up_weight, down_weight):
    rows, width = tokens.shape
    top = route_ids.shape[1]
    groups = lax.axis_size("expert")
    experts = gate_weight.shape[0] * groups
    capacity = min(rows, (5 * top * rows + 4 * experts - 1) // (4 * experts))
    slots = experts * capacity
    piece = (width // 4 + 127) // 128 * 128
    small = width // 2 - piece
    pieces, starts = (small, piece), (0, 2 * small)
    z_pieces, z_starts = (piece, small), (0, 2 * piece)
    at = jnp.stack([lax.axis_index("ffn"), lax.axis_index("dp")]).astype(jnp.int32)

    def swap(x, by, axis="ffn"):
        return lax.ppermute(x, axis, [(i, i ^ by) for i in range(N)])

    def flip(x):
        return lax.ppermute(
            x, ("dp", "ffn"), [(a * N + b, b * N + a) for a in range(N) for b in range(N)]
        )

    def exchange(x):
        return lax.all_to_all(x, "expert", split_axis=0, concat_axis=0, tiled=True)

    def gather_rows(packed):
        received = exchange(packed)
        own = dot(order, received.reshape(2 * slots, -1), NN).astype(BF16).reshape(2, slots, -1)
        near, other = swap(own, 1), swap(own, 3)
        return [own, near, swap(near[0], 3), swap(other[1], 1), other]

    z_local = flip(grad_out)

    to = jnp.arange(2 * slots, dtype=jnp.int32)
    to = to % slots // capacity * (2 * capacity) + to // slots * capacity + to % capacity
    order = (to[:, None] == jnp.arange(2 * slots, dtype=jnp.int32)[None, :]).astype(BF16)
    order_back = (jnp.arange(2 * slots, dtype=jnp.int32)[:, None] == to[None, :]).astype(BF16)

    w_in = jnp.concatenate([gate_weight[0], up_weight[0]], axis=1)
    w_in = lax.all_gather(w_in, "dp", axis=0, tiled=False)

    slot_index = jnp.arange(2 * slots, dtype=jnp.int32)[:, None]

    def hits_of(slot):
        return [[slot_index == (slot[:, k] + c * capacity)[None, :] for k in range(top)] for c in range(2)]

    def one_hot(hits):
        return jnp.concatenate([sum(h.astype(BF16) for h in hit) for hit in hits], axis=1)

    slot = slots_of(route_ids, experts, 2 * capacity)
    x_place = one_hot(hits_of(slot))
    routing = flip(jnp.concatenate([slot.astype(F32), combine], axis=1))
    z_hits = hits_of(routing[:, :top].astype(jnp.int32))
    z_place = one_hot(z_hits)
    z_scale = jnp.zeros((), F32)
    for hit in z_hits:
        for k in range(top):
            z_scale = jnp.where(hit[k], routing[:, top + k][None, :], z_scale)
    z_scale = jnp.sum(z_scale, axis=1)[:, None]

    def stacked(x, lo, w):
        return jnp.concatenate([x[:, lo : lo + w], x[:, lo + w : lo + 2 * w]], axis=0)

    def pack_x(h):
        return dot(x_place, stacked(tokens, starts[h], pieces[h]), NN).astype(BF16).reshape(groups, 2 * capacity, -1)

    def pack_z(h):
        packed = dot(z_place, stacked(z_local, z_starts[h], z_pieces[h]), NN) * z_scale
        return packed.astype(BF16).reshape(groups, 2 * capacity, -1)

    x_0 = gather_rows(pack_x(0))
    z_0 = gather_rows(pack_z(0))
    z_1 = gather_rows(pack_z(1))
    x_1 = gather_rows(pack_x(1))

    partial = hidden_grads((z_0, z_1), down_weight[0], at)
    grads = lax.all_to_all(partial, "dp", split_axis=0, concat_axis=0, tiled=True)
    base = project([(starts[0], (0, 1, 2, 3), x_0), (starts[1], (0, 1, 3), x_1)], w_in, at)
    hidden, acts = project([(starts[1], (2,), x_1)], w_in, at, base, grads)

    part_gate = weight_grad((x_0, x_1), acts, at, 0, unroll=True)
    grad_gate = lax.psum_scatter(part_gate, "dp", scatter_dimension=0, tiled=True)
    grad_gate = grad_gate.astype(F32)
    leads = []
    for h in range(2):
        leads.append(input_partials(acts, w_in, at, starts[h], pieces[h]))
    received = []
    for h in range(2):
        received.append([swap(leads[h][j - 1], j) for j in range(1, N)])
    direct = weight_grad((x_0,), acts, at, gate_weight.shape[2], relative=True)
    scattered = weight_grad((x_1,), acts, at, gate_weight.shape[2])
    scattered = lax.psum_scatter(scattered, "dp", scatter_dimension=0, tiled=True)
    direct = [direct[0]] + [swap(direct[j], j, "dp") for j in range(1, N)]
    direct = sum(d.astype(F32) for d in direct)
    grad_up = jnp.concatenate([direct[None], scattered.astype(F32)], axis=1)

    grad_tokens = []
    hidden, grad_gate = lax.optimization_barrier((hidden, grad_gate))
    hidden_all = lax.all_gather(hidden, "dp", axis=0, tiled=False)
    grad_down = down_grad((z_0, z_1), hidden_all, at)[None]
    for h in range(2):
        total = input_totals(acts, w_in, at, starts[h], received[h], order_back)
        back = exchange(total.reshape(groups, 2 * capacity, -1))
        back = back.reshape(2 * slots, -1)
        if h == 1:
            x_place, grad_down = lax.optimization_barrier((x_place, grad_down))
        back = dot(x_place, back, TN).astype(BF16)
        grad_tokens += [back[:rows], back[rows:]]
    grad_tokens = jnp.concatenate(grad_tokens, axis=1)

    return grad_tokens, grad_gate, grad_up, grad_down


def solution(mesh):
    return jax.shard_map(
        per_device,
        mesh=mesh,
        in_specs=(
            P(("dp", "expert"), "ffn"),
            P(("dp", "expert"), "ffn"),
            P(("dp", "expert"), None),
            P(("dp", "expert"), None),
            P("expert", "dp", "ffn"),
            P("expert", "dp", "ffn"),
            P("expert", "ffn", "dp"),
        ),
        out_specs=(
            P(("dp", "expert"), "ffn"),
            P("expert", "dp", "ffn"),
            P("expert", "dp", "ffn"),
            P("expert", "ffn", "dp"),
        ),
        check_vma=False,
    )
```

```python
import jax
import jax.numpy as jnp
from jax import lax
from jax.experimental import pallas as pl
from jax.experimental.pallas import tpu as pltpu
from jax.sharding import PartitionSpec as P


F32 = jnp.float32
BF16 = jnp.bfloat16
N = 4
ANY = pl.BlockSpec(memory_space=pl.ANY)
SMEM = pl.BlockSpec(memory_space=pltpu.SMEM)


def dot(a, b, contract):
    return lax.dot_general(a, b, (contract, ((), ())), preferred_element_type=F32)


NN, NT, TN = ((1,), (0,)), ((1,), (1,)), ((0,), (0,))


def call(body, outs, scratch, args, copies):
    return pl.pallas_call(
        body,
        out_shape=outs,
        in_specs=[SMEM] + [ANY] * (len(args) - 1),
        out_specs=jax.tree.map(lambda _: ANY, outs),
        scratch_shapes=list(scratch) + [pltpu.SemaphoreType.DMA((copies,))],
    )(*args)


def start(src, dst, sem):
    copy = pltpu.make_async_copy(src, dst, sem)
    copy.start()
    return copy


def slice_of(at, size):
    return pl.ds(at if isinstance(at, int) else pl.multiple_of(at, 128), size)


def place(part, buf, sem):
    if len(part) == 1:
        start(part[0], buf, sem)
    else:
        for c in range(2):
            start(part[c], buf.at[c], sem)


def grouped(refs):
    return [[refs[0]], [refs[1]], [refs[2], refs[3]], [refs[4]]]


PER = N + 1


def vmem(*shape, dtype=BF16):
    return pltpu.VMEM(shape, dtype)


def project(groups, w_in, at, base=None, grads=None):
    rows = groups[0][2][0].shape[1]
    cols = w_in.shape[2]
    units = cols // 2
    last = base is not None
    arrays = [x for _, js, parts in groups for j in js for x in grouped(parts)[j]]
    widths = [parts[0].shape[2] for _, _, parts in groups]
    count = sum(len(js) for _, js, _ in groups)

    def body(at_ref, w_ref, *refs):
        x_refs, refs = refs[: len(arrays)], refs[len(arrays) :]
        if last:
            (base_ref, grad_ref, out_h, out_a), refs = refs[:4], refs[4:]
        else:
            (out,), refs = refs[:1], refs[1:]
        w_bufs, x_bufs, refs = refs[: len(groups)], refs[len(groups) : 2 * len(groups)], refs[2 * len(groups) :]
        total, sems = refs[0], refs[-1]
        array, sem = 0, 0
        for g, (offset, js, parts) in enumerate(groups):
            for i, j in enumerate(js):
                size = len(grouped(parts)[j])
                start(w_ref.at[at_ref[0] ^ j, pl.ds(offset, 2 * widths[g])], w_bufs[g].at[i], sems.at[sem])
                place(x_refs[array : array + size], x_bufs[g].at[i], sems.at[count + sem])
                array, sem = array + size, sem + 1
        if last:
            h_buf, a_buf, grad_buf = refs[1:4]
            first = start(base_ref, total, sems.at[2 * count])
            second = start(grad_ref, grad_buf, sems.at[2 * count + 1])
            first.wait()
        else:
            total[...] = jnp.zeros_like(total)
        sem = 0
        for g, (offset, js, _) in enumerate(groups):
            width, w_buf, x_buf, lo = widths[g], w_bufs[g], x_bufs[g], sem

            def step(i, carry, width=width, w_buf=w_buf, x_buf=x_buf, lo=lo, offset=offset):
                pltpu.make_async_copy(w_ref.at[0, pl.ds(offset, 2 * width)], w_buf.at[i], sems.at[lo + i]).wait()
                pltpu.make_async_copy(x_buf.at[i], x_buf.at[i], sems.at[count + lo + i]).wait()
                total[...] += dot(x_buf[i, 0], w_buf[i, :width], NN) + dot(x_buf[i, 1], w_buf[i, width:], NN)
                return carry

            lax.fori_loop(0, len(js), step, 0)
            sem += len(js)
        if last:
            second.wait()
            grad = sum(grad_buf[j].astype(F32) for j in range(N))
            gate, up = total[:, :units], total[:, units:]
            sig = jax.nn.sigmoid(gate)
            h_buf[...] = (gate * sig * up).astype(BF16)
            a_buf[:, :units] = (grad * up * sig * (1.0 + gate * (1.0 - sig))).astype(BF16)
            a_buf[:, units:] = (grad * gate * sig).astype(BF16)
            stores = [start(h_buf, out_h, sems.at[0]), start(a_buf, out_a, sems.at[1])]
        else:
            stores = [start(total, out, sems.at[0])]
        for copy in stores:
            copy.wait()

    scratch = [vmem(len(js), 2 * w, cols) for (_, js, _), w in zip(groups, widths)]
    scratch += [vmem(len(js), 2, rows, w) for (_, js, _), w in zip(groups, widths)] + [vmem(rows, cols, dtype=F32)]
    if not last:
        return call(body, jax.ShapeDtypeStruct((rows, cols), F32), scratch, [at, w_in] + arrays, 2 * count)
    outs = (jax.ShapeDtypeStruct((rows, units), BF16), jax.ShapeDtypeStruct((rows, cols), BF16))
    scratch += [vmem(rows, units), vmem(rows, cols), vmem(N, rows, units)]
    return call(body, outs, scratch, [at, w_in] + arrays + [base, grads], 2 * count + 2)


def fetch(chunks, x_refs, x_bufs, sems, base):
    for j in range(N):
        for h in range(len(chunks)):
            place(grouped(x_refs[h * PER :])[j], x_bufs[h].at[j], sems.at[base + h * N + j])


def arrived(x_refs, x_bufs, sems, base, h, j):
    pltpu.make_async_copy(x_refs[h * PER], x_bufs[h].at[j], sems.at[base + h * N + j]).wait()


def flat(chunks):
    return [x for parts in chunks for x in parts]


def buffers(chunks):
    return [vmem(N, *parts[0].shape) for parts in chunks]


def hidden_grads(chunks, w_down, at):
    rows = chunks[0][0].shape[1]
    units, width = w_down.shape
    count = len(chunks)

    def body(at_ref, w_ref, *refs):
        x_refs, (out, w_buf, *x_bufs, out_buf, sems) = refs[: count * PER], refs[count * PER :]
        first = start(w_ref, w_buf, sems.at[0])
        fetch(chunks, x_refs, x_bufs, sems, 1 + N)
        first.wait()

        def step(j, carry):
            total, lo = None, 0
            for h in range(count):
                w = x_bufs[h].shape[3]
                arrived(x_refs, x_bufs, sems, 1 + N, h, j)
                for c in range(2):
                    term = dot(x_bufs[h][j, c], w_buf[:, lo : lo + w], NT)
                    total = term if total is None else total + term
                    lo += w
            out_buf[j] = total.astype(BF16)
            start(out_buf.at[j], out.at[at_ref[0] ^ j], sems.at[1 + j])
            return carry

        lax.fori_loop(0, N, step, 0)
        for j in range(N):
            pltpu.make_async_copy(out_buf.at[j], out.at[0], sems.at[1 + j]).wait()

    scratch = [vmem(units, width)] + buffers(chunks) + [vmem(N, rows, units)]
    out = jax.ShapeDtypeStruct((N, rows, units), BF16)
    return call(body, out, scratch, [at, w_down] + flat(chunks), 1 + N + count * N)


def weight_grad(chunks, acts, at, lo_col, unroll=False):
    rows, cols = acts.shape
    units = cols // 2
    width = sum(2 * parts[0].shape[2] for parts in chunks)
    count = len(chunks)

    def body(at_ref, a_ref, *refs):
        x_refs, (out, a_buf, *x_bufs, out_buf, sems) = refs[: count * PER], refs[count * PER :]
        first = start(a_ref, a_buf, sems.at[0])
        fetch(chunks, x_refs, x_bufs, sems, 1 + N)
        first.wait()

        def step(j, carry):
            lo = 0
            for h in range(count):
                w = x_bufs[h].shape[3]
                arrived(x_refs, x_bufs, sems, 1 + N, h, j)

                def piece(c, carry, h=h, lo=lo, w=w):
                    grads = dot(x_bufs[h][j, c], a_buf[:, lo_col : lo_col + units], TN)
                    out_buf[j, slice_of(lo + c * w, w)] = grads.astype(BF16)
                    return carry

                if unroll:
                    for c in range(2):
                        piece(c, 0)
                else:
                    lax.fori_loop(0, 2, piece, 0)
                lo += 2 * w
            start(out_buf.at[j], out.at[at_ref[0] ^ j], sems.at[1 + j])
            return carry

        lax.fori_loop(0, N, step, 0)
        for j in range(N):
            pltpu.make_async_copy(out_buf.at[j], out.at[0], sems.at[1 + j]).wait()

    scratch = [vmem(rows, cols)] + buffers(chunks) + [vmem(N, width, units)]
    out = jax.ShapeDtypeStruct((N, width, units), BF16)
    return call(body, out, scratch, [at, acts] + flat(chunks), 1 + N + count * N)


def down_grad(chunks, hidden, at):
    _, rows, units = hidden.shape
    width = sum(2 * parts[0].shape[2] for parts in chunks)
    count = len(chunks)

    def body(at_ref, h_ref, *refs):
        x_refs, (out, h_buf, *x_bufs, out_buf, sems) = refs[: count * PER], refs[count * PER :]
        first = start(h_ref, h_buf, sems.at[0])
        fetch(chunks, x_refs, x_bufs, sems, 1)
        out_buf[...] = jnp.zeros_like(out_buf)
        first.wait()

        def step(j, carry):
            lo = 0
            for h in range(count):
                w = x_bufs[h].shape[3]
                arrived(x_refs, x_bufs, sems, 1, h, j)

                def piece(c, carry, h=h, lo=lo, w=w):
                    out_buf[:, pl.ds(pl.multiple_of(lo + c * w, 128), w)] += dot(
                        h_buf[at_ref[0] ^ j], x_bufs[h][j, c], TN
                    )
                    return carry

                lax.fori_loop(0, 2, piece, 0)
                lo += 2 * w
            return carry

        lax.fori_loop(0, N, step, 0)
        start(out_buf, out, sems.at[0]).wait()

    scratch = [vmem(N, rows, units)] + buffers(chunks) + [vmem(units, width, dtype=F32)]
    out = jax.ShapeDtypeStruct((units, width), F32)
    return call(body, out, scratch, [at, hidden] + flat(chunks), 1 + count * N)


def input_partials(acts, w_in, at, offset, width):
    rows, cols = acts.shape

    def body(at_ref, a_ref, w_ref, *refs):
        outs, (a_buf, w_buf, out_buf, sems) = refs[: N - 1], refs[N - 1 :]
        first = start(a_ref, a_buf, sems.at[0])
        for j in range(1, N):
            start(w_ref.at[at_ref[0] ^ j, pl.ds(offset, 2 * width)], w_buf.at[j - 1], sems.at[j])
        first.wait()

        def step(j, carry):
            pltpu.make_async_copy(w_ref.at[0, pl.ds(offset, 2 * width)], w_buf.at[j], sems.at[1 + j]).wait()

            for c in range(2):
                out_buf[j, c] = dot(a_buf[...], w_buf[j, c * width : (c + 1) * width], NT).astype(BF16)
            return carry

        lax.fori_loop(0, N - 1, step, 0)
        stores = [start(out_buf.at[j], outs[j], sems.at[j]) for j in range(N - 1)]
        for copy in stores:
            copy.wait()

    outs = (jax.ShapeDtypeStruct((2, rows, width), BF16),) * (N - 1)
    scratch = [vmem(rows, cols), vmem(N - 1, 2 * width, cols), vmem(N - 1, 2, rows, width)]
    return call(body, outs, scratch, [at, acts, w_in], N)


def input_totals(acts, w_in, at, offset, received, order):
    rows, cols = acts.shape
    _, _, width = received[0].shape

    def body(at_ref, a_ref, w_ref, order_ref, *refs):
        r_refs, (out, a_buf, w_buf, o_buf, r_buf, t_buf, out_buf, sems) = refs[: N - 1], refs[N - 1 :]
        copies = [
            start(a_ref, a_buf, sems.at[0]),
            start(w_ref.at[at_ref[0], pl.ds(offset, 2 * width)], w_buf, sems.at[1]),
            start(order_ref, o_buf, sems.at[2]),
        ]
        copies += [start(r_refs[j], r_buf.at[j], sems.at[3 + j]) for j in range(N - 1)]
        for copy in copies:
            copy.wait()

        for c in range(2):
            total = dot(a_buf[...], w_buf[c * width : (c + 1) * width], NT)
            for j in range(N - 1):
                total = total + r_buf[j, c].astype(F32)
            t_buf[c * rows : (c + 1) * rows] = total.astype(BF16)

        def step(i, carry):
            block = pl.ds(i * (rows // 2), rows // 2)
            out_buf[block] = dot(o_buf[block], t_buf[...], NN).astype(BF16)
            return carry

        lax.fori_loop(0, 4, step, 0)
        start(out_buf, out, sems.at[0]).wait()

    scratch = [vmem(rows, cols), vmem(2 * width, cols), vmem(2 * rows, 2 * rows), vmem(N - 1, 2, rows, width)]
    scratch += [vmem(2 * rows, width), vmem(2 * rows, width)]
    out = jax.ShapeDtypeStruct((2 * rows, width), BF16)
    return call(body, out, scratch, [at, acts, w_in, order] + list(received), 3 + N - 1)


def slots_of(route, experts, stride):
    rows, top = route.shape
    expert_of = route.reshape(rows * top)
    onehot = (expert_of[:, None] == jnp.arange(experts, dtype=jnp.int32)[None, :]).astype(jnp.int32)
    earlier = jnp.cumsum(onehot, axis=0) - onehot
    position = jnp.sum(earlier * onehot, axis=1)
    return (expert_of * stride + position).reshape(rows, top)


def per_device(tokens, grad_out, route_ids, combine, gate_weight, up_weight, down_weight):
    rows, width = tokens.shape
    top = route_ids.shape[1]
    groups = lax.axis_size("expert")
    experts = gate_weight.shape[0] * groups
    capacity = min(rows, (5 * top * rows + 4 * experts - 1) // (4 * experts))
    slots = experts * capacity
    piece = (width // 4 + 127) // 128 * 128
    small = width // 2 - piece
    pieces, starts = (small, piece), (0, 2 * small)
    z_pieces, z_starts = (piece, small), (0, 2 * piece)
    at = lax.axis_index("ffn").astype(jnp.int32)[None]

    def swap(x, by):
        return lax.ppermute(x, "ffn", [(i, i ^ by) for i in range(N)])

    def flip(x):
        return lax.ppermute(
            x, ("dp", "ffn"), [(a * N + b, b * N + a) for a in range(N) for b in range(N)]
        )

    def exchange(x):
        return lax.all_to_all(x, "expert", split_axis=0, concat_axis=0, tiled=True)

    def gather_rows(packed):
        received = exchange(packed)
        own = dot(order, received.reshape(2 * slots, -1), NN).astype(BF16).reshape(2, slots, -1)
        near, other = swap(own, 1), swap(own, 3)
        return [own, near, swap(near[0], 3), swap(other[1], 1), other]

    z_local = flip(grad_out)

    to = jnp.arange(2 * slots, dtype=jnp.int32)
    to = to % slots // capacity * (2 * capacity) + to // slots * capacity + to % capacity
    order = (to[:, None] == jnp.arange(2 * slots, dtype=jnp.int32)[None, :]).astype(BF16)
    order_back = (jnp.arange(2 * slots, dtype=jnp.int32)[:, None] == to[None, :]).astype(BF16)

    w_in = jnp.concatenate([gate_weight[0], up_weight[0]], axis=1)
    w_in = lax.all_gather(w_in, "dp", axis=0, tiled=False)

    slot_index = jnp.arange(2 * slots, dtype=jnp.int32)[:, None]

    def hits_of(slot):
        return [[slot_index == (slot[:, k] + c * capacity)[None, :] for k in range(top)] for c in range(2)]

    def one_hot(hits):
        return jnp.concatenate([sum(h.astype(BF16) for h in hit) for hit in hits], axis=1)

    slot = slots_of(route_ids, experts, 2 * capacity)
    x_place = one_hot(hits_of(slot))
    routing = flip(jnp.concatenate([slot.astype(F32), combine], axis=1))
    z_hits = hits_of(routing[:, :top].astype(jnp.int32))
    z_place = one_hot(z_hits)
    z_scale = jnp.zeros((), F32)
    for hit in z_hits:
        for k in range(top):
            z_scale = jnp.where(hit[k], routing[:, top + k][None, :], z_scale)
    z_scale = jnp.sum(z_scale, axis=1)[:, None]

    def stacked(x, lo, w):
        return jnp.concatenate([x[:, lo : lo + w], x[:, lo + w : lo + 2 * w]], axis=0)

    def pack_x(h):
        return dot(x_place, stacked(tokens, starts[h], pieces[h]), NN).astype(BF16).reshape(groups, 2 * capacity, -1)

    def pack_z(h):
        packed = dot(z_place, stacked(z_local, z_starts[h], z_pieces[h]), NN) * z_scale
        return packed.astype(BF16).reshape(groups, 2 * capacity, -1)

    x_0 = gather_rows(pack_x(0))
    z_0 = gather_rows(pack_z(0))
    z_1 = gather_rows(pack_z(1))
    x_1 = gather_rows(pack_x(1))

    partial = hidden_grads((z_0, z_1), down_weight[0], at)
    grads = lax.all_to_all(partial, "dp", split_axis=0, concat_axis=0, tiled=True)
    base = project([(starts[0], (0, 1, 2, 3), x_0), (starts[1], (0, 1, 3), x_1)], w_in, at)
    hidden, acts = project([(starts[1], (2,), x_1)], w_in, at, base, grads)

    part_gate = weight_grad((x_0, x_1), acts, at, 0, unroll=True)
    grad_gate = lax.psum_scatter(part_gate, "dp", scatter_dimension=0, tiled=True)
    grad_gate = grad_gate.astype(F32)
    leads = []
    for h in range(2):
        leads.append(input_partials(acts, w_in, at, starts[h], pieces[h]))
    received = []
    for h in range(2):
        received.append([swap(leads[h][j - 1], j) for j in range(1, N)])
    part_up = weight_grad((x_0, x_1), acts, at, gate_weight.shape[2])
    grad_up = lax.psum_scatter(part_up, "dp", scatter_dimension=0, tiled=True).astype(F32)

    grad_tokens = []
    hidden_all = lax.all_gather(hidden, "dp", axis=0, tiled=False)
    received[1], hidden_all = lax.optimization_barrier((received[1], hidden_all))
    hidden_all, grad_gate = lax.optimization_barrier((hidden_all, grad_gate))
    grad_down = down_grad((z_0, z_1), hidden_all, at)[None]
    for h in range(2):
        total = input_totals(acts, w_in, at, starts[h], received[h], order_back)
        back = exchange(total.reshape(groups, 2 * capacity, -1))
        back = back.reshape(2 * slots, -1)
        if h == 1:
            x_place, grad_down = lax.optimization_barrier((x_place, grad_down))
        back = dot(x_place, back, TN).astype(BF16)
        grad_tokens += [back[:rows], back[rows:]]
    grad_tokens = jnp.concatenate(grad_tokens, axis=1)

    return grad_tokens, grad_gate, grad_up, grad_down


def solution(mesh):
    return jax.shard_map(
        per_device,
        mesh=mesh,
        in_specs=(
            P(("dp", "expert"), "ffn"),
            P(("dp", "expert"), "ffn"),
            P(("dp", "expert"), None),
            P(("dp", "expert"), None),
            P("expert", "dp", "ffn"),
            P("expert", "dp", "ffn"),
            P("expert", "ffn", "dp"),
        ),
        out_specs=(
            P(("dp", "expert"), "ffn"),
            P("expert", "dp", "ffn"),
            P("expert", "dp", "ffn"),
            P("expert", "ffn", "dp"),
        ),
        check_vma=False,
    )
```
